32 devices in a mesh: head: 4 (over y, x), ctx: 8 (over z, core).
Axes of the slice: x: 2, y: 2, z: 4, core: 2. Of those that a mesh axis runs over, the one named last changes fastest.
Arguments:
- query_rows: bfloat16 [4096, 2048], P(('ctx', 'head')), may hold values from -6 to 6
- key_rows: bfloat16 [4096, 2048], P(('ctx', 'head')), may hold values from -6 to 6
- value_rows: bfloat16 [4096, 4096], P(('ctx', 'head')), may hold values from -6 to 6
- gate_rows: bfloat16 [4096, 4096], P(('ctx', 'head')), may hold values from -6 to 6
- write_strength: bfloat16 [4096, 32], P(('ctx', 'head')), may hold values from 0 to 1
- log_decay: bfloat16 [4096, 32], P(('ctx', 'head')), may hold values from -1 to 0
- norm_gain: float32 [128], replicated, may hold values from 0.1 to 1.9
Outputs:
- mixed_out: bfloat16 [4096, 4096], P(('ctx', 'head'))
The draws below stay inside these ranges and needn't reach their ends.
All inputs are finite; a program needn't handle non-finite values.
Results may differ from the reference program's by a relative error of at most 0.0049.
Values may be sent and summed in bfloat16 or wider, within the bound.
A program may use at most 192 MiB of HBM per device.

```python
import math
import jax
import jax.numpy as jnp
from jax import lax

HK = 16
VALUE_HEADS = 32
DK = 128
DV = 128
C = 64
SEQUENCE_TOKENS = 4096


def head_kinds(key):
    picker = jax.random.fold_in(key, 11)
    fast = jax.random.randint(picker, (VALUE_HEADS,), 0, 2) == 1
    return fast


def draw_write_strength(key, part):
    fast = head_kinds(key)
    first, second, third = jax.random.split(jax.random.fold_in(key, 21), 3)
    fast_beta = jax.random.uniform(first, (SEQUENCE_TOKENS, VALUE_HEADS), jnp.float32, 0.2, 1.0)
    slow_level = jnp.exp(jax.random.uniform(second, (VALUE_HEADS,), jnp.float32, math.log(0.3), 0.0)) * DK / SEQUENCE_TOKENS
    slow_beta = slow_level[None, :] * jax.random.uniform(third, (SEQUENCE_TOKENS, VALUE_HEADS), jnp.float32, 0.5, 2.0)
    return jnp.where(fast[None, :], fast_beta, slow_beta).astype(jnp.bfloat16)


def draw_log_decay(key, part):
    fast = head_kinds(key)
    first, second, third, fourth_factor, fifth_factor = jax.random.split(jax.random.fold_in(key, 31), 5)
    fast_rate = jnp.exp(jax.random.uniform(first, (VALUE_HEADS,), jnp.float32, math.log(1.0 / 50.0), math.log(1.0 / 30.0)))
    slow_rate = jnp.exp(jax.random.uniform(second, (VALUE_HEADS,), jnp.float32, math.log(0.1), math.log(0.4))) / SEQUENCE_TOKENS
    decay_speed = jnp.where(fast, fast_rate, slow_rate)
    coarse_estimate = jax.random.uniform(third, (SEQUENCE_TOKENS, VALUE_HEADS), jnp.float32, 0.5, 2.0)
    token_group = jax.random.randint(fourth_factor, (SEQUENCE_TOKENS, VALUE_HEADS), 0, SEQUENCE_TOKENS // 2) == 0
    token_group_length = jax.random.uniform(fifth_factor, (SEQUENCE_TOKENS, VALUE_HEADS), jnp.float32, 0.22, 0.69)
    return (-(decay_speed[None, :] * coarse_estimate + jnp.where(token_group, token_group_length, 0.0))).astype(jnp.bfloat16)


def levels(own_key, extent, cuts, least, top_value):
    def one(axis_at, shards_of):
        heights = jax.random.uniform(jax.random.fold_in(jax.random.fold_in(own_key, 6), axis_at), (shards_of,), jnp.float32, least / len(cuts), top_value / len(cuts))
        return jnp.repeat(jnp.exp(heights), extent[axis_at] // shards_of).reshape((-1,) + (1,) * (len(extent) - axis_at - 1))

    factor_of = one(*cuts[0])
    for cut in cuts[1:]:
        factor_of = factor_of * one(*cut)
    return factor_of


def gaussian(key, shape, deviation, bound, shards=(), held_as=jnp.bfloat16):
    values = deviation * jax.random.normal(key, shape, jnp.float32)
    if shards:
        values = values * levels(key, shape, shards, -0.22, 0.18)
    return jnp.clip(values, -bound, bound).astype(held_as)


def setup_inputs(seed: int = 0) -> dict:
    keys = jax.random.split(jax.random.key(seed), 8)
    query_rows = gaussian(keys[0], (SEQUENCE_TOKENS, HK * DK), 1.0, 6.0, ((0, 32),))
    key_rows = gaussian(keys[1], (SEQUENCE_TOKENS, HK * DK), 1.0, 6.0, ((0, 32),))
    value_rows = gaussian(keys[2], (SEQUENCE_TOKENS, VALUE_HEADS * DV), 1.0, 6.0, ((0, 32),))
    gate_rows = gaussian(keys[3], (SEQUENCE_TOKENS, VALUE_HEADS * DV), 1.0, 6.0, ((0, 32),))
    write_strength = draw_write_strength(jax.random.fold_in(keys[7], 71), 0)
    log_decay = draw_log_decay(jax.random.fold_in(keys[7], 71), 0)
    norm_gain = jnp.clip(1.0 + 0.18 * jax.random.normal(keys[6], (DV,), jnp.float32), 0.1, 1.9)
    return {"query_rows": query_rows, "key_rows": key_rows, "value_rows": value_rows, "gate_rows": gate_rows, "write_strength": write_strength, "log_decay": log_decay, "norm_gain": norm_gain}


def unit_rows(vectors):
    return vectors * lax.rsqrt(lax.optimization_barrier(jnp.sum(vectors * vectors, axis=-1, keepdims=True)) + 1e-06)

def unit_lower_apply(system_off, right_hand):
    highest = lax.Precision.HIGHEST
    group_len = system_off.shape[-1]
    rounds = (group_len - 1).bit_length()
    power = -system_off
    solved = right_hand
    for index in range(rounds):
        solved = solved + jnp.einsum('...ij,...jk->...ik', power, solved, precision=highest)
        if index + 1 < rounds:
            power = jnp.einsum('...ij,...jk->...ik', power, power, precision=highest)
    return solved

def group_terms(query_blk, key_blk, value_blk, beta_blk, decay_blk):
    highest = lax.Precision.HIGHEST
    group_len = query_blk.shape[-2]
    cumulative = jnp.cumsum(decay_blk, axis=-1)
    gaps_log = cumulative[..., :, None] - cumulative[..., None, :]
    position = jnp.arange(group_len)
    causal = position[:, None] >= position[None, :]
    strict = position[:, None] > position[None, :]
    weights = jnp.where(causal, jnp.exp(jnp.minimum(gaps_log, 0.0)), 0.0)
    key_inner = jnp.einsum('...id,...jd->...ij', key_blk, key_blk, precision=highest)
    system_off = jnp.where(strict, beta_blk[..., :, None] * weights * key_inner, 0.0)
    growth = jnp.exp(cumulative)
    right_hand = jnp.concatenate([beta_blk[..., None] * value_blk, (beta_blk * growth)[..., None] * key_blk], axis=-1)
    solved = unit_lower_apply(system_off, right_hand)
    value_width = value_blk.shape[-1]
    fresh_vals = solved[..., :value_width]
    key_factor = solved[..., value_width:]
    to_end = jnp.exp(cumulative[..., -1:] - cumulative)
    key_scaled = to_end[..., None] * key_blk
    identity = jnp.eye(key_blk.shape[-1], dtype=jnp.float32)
    transition = growth[..., -1, None, None] * identity - jnp.einsum('...cd,...ce->...de', key_scaled, key_factor, precision=highest)
    written = jnp.einsum('...cd,...ce->...de', key_scaled, fresh_vals, precision=highest)
    scores = jnp.einsum('...id,...jd->...ij', query_blk, key_blk, precision=highest) * weights
    local_out = jnp.einsum('...ij,...je->...ie', scores, fresh_vals, precision=highest)
    reader = growth[..., None] * query_blk - jnp.einsum('...ij,...jd->...id', scores, key_factor, precision=highest)
    return (transition, written, reader, local_out)

def gated_norm(core, gate_rows, norm_gain):
    values = lax.optimization_barrier(core).astype(jnp.float32)
    values = values.reshape(core.shape[0], -1, norm_gain.shape[0])
    scaled = values * lax.rsqrt(lax.optimization_barrier(jnp.mean(values * values, axis=-1, keepdims=True)) + 1e-06)
    gates = gate_rows.astype(jnp.float32).reshape(values.shape)
    result = scaled * norm_gain * jax.nn.silu(gates)
    return result.reshape(core.shape[0], -1).astype(jnp.bfloat16)

def reference(query_rows, key_rows, value_rows, gate_rows, write_strength, log_decay, norm_gain):
    highest = lax.Precision.HIGHEST
    seq_len = query_rows.shape[0]
    queries = jnp.repeat(unit_rows(query_rows.astype(jnp.float32).reshape(seq_len, HK, DK)), VALUE_HEADS // HK, axis=1)
    keys_all = jnp.repeat(unit_rows(key_rows.astype(jnp.float32).reshape(seq_len, HK, DK)), VALUE_HEADS // HK, axis=1)
    values = value_rows.astype(jnp.float32).reshape(seq_len, VALUE_HEADS, DV)
    strength = write_strength.astype(jnp.float32)
    decay_log = log_decay.astype(jnp.float32)
    blocks = seq_len // C

    def blocked(array):
        return jnp.swapaxes(array.reshape((blocks, C) + array.shape[1:]), 1, 2)

    def advance(state, inputs):
        transition, written, reader, local_out = group_terms(*inputs)
        output = local_out + jnp.einsum('hcd,hde->hce', reader, state, precision=highest)
        state = jnp.einsum('hde,hef->hdf', transition, state, precision=highest) + written
        return (state, output)
    start_state = jnp.zeros((VALUE_HEADS, DK, DV), jnp.float32)
    final_state, outputs = lax.scan(advance, start_state, (blocked(queries), blocked(keys_all), blocked(values), blocked(strength), blocked(decay_log)))
    core = jnp.swapaxes(outputs, 1, 2).reshape(seq_len, VALUE_HEADS * DV).astype(jnp.bfloat16)
    return gated_norm(core, gate_rows, norm_gain)
```

```python
import functools

import jax
import jax.numpy as jnp
from jax import lax
from jax.experimental import pallas as pl
from jax.experimental.pallas import tpu as pltpu
from jax.sharding import PartitionSpec as P

D = 128
B = 128
F32 = jnp.float32
BF = jnp.bfloat16
MESH = pl.DeviceIdType.MESH


def split(x):
    hi = x.astype(BF)
    return hi, (x - hi.astype(F32)).astype(BF)


def dot(a, b):
    return jnp.dot(a, b, preferred_element_type=F32)


def dot_t(a, b):
    return lax.dot_general(a, b, (((1,), (1,)), ((), ())), preferred_element_type=F32)


def dot_b(a, b):
    return dot(a.astype(BF), b.astype(BF))


def dot_fe(a, b):
    hi, lo = split(a)
    return dot(jnp.concatenate([hi, lo], 1), jnp.concatenate([b, b], 0))


def dot_ef(a, b):
    hi, lo = split(b)
    return dot(jnp.concatenate([a, a], 1), jnp.concatenate([hi, lo], 0))


def dot_sf(ah, al, b):
    bh, bl = split(b)
    return dot(jnp.concatenate([ah, ah], 1), jnp.concatenate([bh, bl], 0)) + dot(al, bh)


def dot_ff(a, b):
    return dot_sf(*split(a), b)


def unit_lower_inverse(lows, ii, jj):
    eye = (ii == jj).astype(F32)

    def same(w):
        return (ii // w) == (jj // w)

    base = same(16)
    p = [jnp.where(base, -x, 0.0) for x in lows]
    t = [eye + x for x in p]
    for _ in range(3):
        pb = [x.astype(BF) for x in p]
        p = [dot(x, x) for x in pb]
        t = [y + dot_b(y, x) for y, x in zip(t, p)]
    w = 16
    while w < B:
        off = same(2 * w) & ~same(w)
        tb = [y.astype(BF) for y in t]
        z = [dot(jnp.where(off, x, 0.0).astype(BF), y) for x, y in zip(lows, tb)]
        t = [y - dot(yb, x.astype(BF)) for y, yb, x in zip(t, tb, z)]
        w *= 2
    return t


def fused_kernel(
    n, m, pair, kheads, per,
    q, k, v, be, de, gate_hbm, gain,
    out,
    qb, kb, vb, beb, deb, gate, ivs, uw, wr, th, tl, ktb, ends, grows, xsb, xh, xf, base, r, sin, sout, core, got,
    es, er, el, fs, fr, fl, gs, cs, cr, ss, rs,
):
    hx = lax.axis_index("head")
    c = lax.axis_index("ctx")
    group = n * pair
    z = c // pair
    me = lax.rem(c, pair) * n + hx
    zs = m // pair
    heads = kheads * per
    t = q.shape[0]
    wide = be.shape[0]
    tb = t // B
    blocks = t * group // B
    half = blocks // 2

    def peer(s):
        rank = lax.rem(me + s, group)
        return {"ctx": z * pair + rank // n, "head": lax.rem(rank, n)}, rank

    barrier = pltpu.get_barrier_semaphore()
    for s in range(1, group):
        pl.semaphore_signal(barrier, inc=1, device_id=peer(s)[0], device_id_type=MESH)
    for s in (pair, m - pair):
        pl.semaphore_signal(barrier, inc=1, device_id={"ctx": lax.rem(c + s, m)}, device_id_type=MESH)
    pl.semaphore_wait(barrier, group + 1)

    mine = pl.ds(pl.multiple_of(me * t, t), t)
    small = ((de, deb), (be, beb))
    large = ((k, kb, D), (v, vb, per * D), (q, qb, D))

    def small_copy(i, s):
        return pltpu.make_async_remote_copy(
            src_ref=small[i][0],
            dst_ref=small[i][1].at[me],
            send_sem=fs.at[i, s],
            recv_sem=fr.at[i, s],
            device_id=peer(s)[0],
            device_id_type=MESH,
        )

    def small_local(i):
        return pltpu.make_async_copy(small[i][0], small[i][1].at[me], fl.at[i])

    def piece(i, a, dest):
        w = large[i][2]
        return large[i][0].at[:, pl.ds(pl.multiple_of((dest * kheads + a) * w, w), w)]

    def large_copy(i, a, s):
        device, dest = peer(s)
        return pltpu.make_async_remote_copy(
            src_ref=piece(i, a, dest),
            dst_ref=large[i][1].at[a, mine, :],
            send_sem=es.at[i, a, s],
            recv_sem=er.at[i, a, s],
            device_id=device,
            device_id_type=MESH,
        )

    def large_local(i, a):
        return pltpu.make_async_copy(piece(i, a, me), large[i][1].at[a, mine, :], el.at[i, a])

    def arrive(i, a):
        for s in range(1, group):
            large_copy(i, a, s).wait_recv()
        large_local(i, a).wait()

    for i in range(2):
        for s in range(1, group):
            small_copy(i, s).start()
        small_local(i).start()
    for i in range(3):
        for a in range(kheads):
            for s in range(1, group):
                large_copy(i, a, s).start()
            large_local(i, a).start()
    gate_copy = pltpu.make_async_copy(gate_hbm, gate, gs)
    gate_copy.start()

    ii = lax.broadcasted_iota(jnp.int32, (B, B), 0)
    jj = lax.broadcasted_iota(jnp.int32, (B, B), 1)
    eye = ii == jj
    causal = ii >= jj
    strict = ii > jj
    low = causal.astype(BF)
    upp = (ii <= jj).astype(BF)
    after = (ii < jj).astype(BF)
    ones = jnp.ones((B, B), BF)
    for i in range(2):
        for s in range(1, group):
            small_copy(i, s).wait_recv()
        small_local(i).wait()

    def block_rows(blk):
        return pl.ds(pl.multiple_of(blk * B, B), B)

    def by_keys(a, hf):
        first = (me * kheads + a) * per
        sel_t = (
            lax.broadcasted_iota(jnp.int32, (8, wide), 1)
            == lax.broadcasted_iota(jnp.int32, (8, wide), 0) + first
        ).astype(BF)
        lows, rights, info = [], [], []
        for b in range(half):
            blk = hf * half + b
            x = a * blocks + blk
            here = pl.ds(0, B) if tb == 1 else pl.ds(pl.multiple_of(lax.rem(blk, tb) * B, B), B)
            drow = dot(sel_t, deb[blk // tb, :, here]).astype(BF)
            berow = dot(sel_t, beb[blk // tb, :, here])
            bcol = dot_t(low, drow)
            brow = dot(drow, upp)
            becol = dot_t(eye.astype(BF), berow.astype(BF))
            grow = jnp.exp(brow)
            lastcol = jnp.exp(dot_t(ones, drow))
            kk = kb[a, block_rows(blk), :]
            g = dot_t(kk, kk)
            diag = jnp.where(eye, g, 0.0)
            rc = lax.rsqrt(jnp.sum(diag, axis=1, keepdims=True) + 1e-6)
            rr = lax.rsqrt(jnp.sum(diag, axis=0, keepdims=True) + 1e-6)
            ecol = jnp.exp(dot_t(after, drow)) * rc
            gn = g * rc * rr
            kt = jnp.transpose(kk)
            ktb[x] = kt
            ends[x] = ecol
            grows[x] = jnp.exp(bcol)
            for u in range(per):
                gap = bcol[:, u : u + 1] - brow[u : u + 1, :]
                wts = jnp.where(causal, jnp.exp(jnp.minimum(gap, 0.0)), 0.0)
                lows.append(jnp.where(strict, becol[:, u : u + 1] * wts * gn, 0.0))
                wr[x * per + u] = wts * rr
                br = berow[u : u + 1, :]
                rights.append((br, br * grow[u : u + 1, :] * rr))
                info.append((x * per + u, kk, kt, lastcol[:, u : u + 1], ecol[:, u : u + 1]))
        inv = unit_lower_inverse(lows, ii, jj)
        for y, (br, bgr), (e, kk, kt, last, end) in zip(inv, rights, info):
            ivs[e] = jnp.concatenate(split(y * br), 1)
            w = dot_fe(y * bgr, kk)
            uw[e, :, D:] = w
            trans = jnp.where(eye, last, 0.0) - dot_ef(kt, end * w)
            th[e], tl[e] = split(trans)

    zero = jnp.zeros((B, D), F32)

    def by_values(a, hf):
        xs = [None] * per
        for b in range(half):
            blk = hf * half + b
            x = a * blocks + blk
            for u in range(per):
                e = x * per + u
                vv = vb[a, block_rows(blk), u * D : (u + 1) * D]
                fresh = dot(ivs[e], jnp.concatenate([vv, vv], 0))
                uw[e, :, :D] = fresh
                written = dot_ef(ktb[x], ends[x][:, u : u + 1] * fresh)
                if b == 0:
                    now = jnp.concatenate([written, th[e].astype(F32) + tl[e].astype(F32)], 1)
                else:
                    now = dot_sf(th[e], tl[e], xs[u]) + jnp.concatenate([written, zero], 1)
                xs[u] = now
                if b < half - 1:
                    xsb[e] = jnp.concatenate(split(now), 0)
        for u in range(per):
            xh[(a * per + u) * 2 + hf] = xs[u]

    def whole_map(a):
        for u in range(per):
            h = a * per + u
            late = xh[h * 2 + 1]
            xf[h] = dot_ff(late[:, D:], xh[h * 2]) + jnp.concatenate([late[:, :D], zero], 1)

    def by_queries(a, hf):
        for b in range(half):
            blk = hf * half + b
            x = a * blocks + blk
            rows = block_rows(blk)
            qq = qb[a, rows, :]
            qf = qq.astype(F32)
            qc = lax.rsqrt(jnp.sum(qf * qf, axis=1, keepdims=True) + 1e-6)
            hn = dot_t(qq, kb[a, rows, :]) * qc
            qn = qf * qc
            for u in range(per):
                e = x * per + u
                lr = dot_ef((wr[e] * hn).astype(BF), uw[e])
                near = lr[:, :D]
                far = (grows[x][:, u : u + 1] * qn - lr[:, D:]).astype(BF)
                if b > 0:
                    o = dot(jnp.concatenate([far, far], 1), xsb[e - per])
                    near = near + o[:, :D]
                    far = o[:, D:].astype(BF)
                base[a * per + u, rows, :] = near
                r[a * per + u, rows, :] = far

    def chain(h):
        return pltpu.make_async_remote_copy(
            src_ref=sout.at[h],
            dst_ref=sin.at[h],
            send_sem=cs.at[h],
            recv_sem=cr.at[h],
            device_id={"ctx": lax.rem(c + pair, m)},
            device_id_type=MESH,
        )

    def send(h, s):
        device, dest = peer(s)
        return pltpu.make_async_remote_copy(
            src_ref=core.at[h, pl.ds(pl.multiple_of(dest * t, t), t), :],
            dst_ref=got.at[me * heads + h],
            send_sem=ss.at[h, s],
            recv_sem=rs.at[h, s],
            device_id=device,
            device_id_type=MESH,
        )

    def pass_on(a):
        for u in range(per):
            h = a * per + u

            @pl.when(z == 0)
            def _():
                sin[h] = jnp.zeros((D, D), F32)
                sout[h] = xf[h, :, :D]

            @pl.when(z > 0)
            def _():
                chain(h).wait_recv()

                @pl.when(z < zs - 1)
                def _():
                    sout[h] = dot_ff(xf[h, :, D:], sin[h]) + xf[h, :, :D]

            @pl.when(z < zs - 1)
            def _():
                chain(h).start()

    def finish(a):
        for u in range(per):
            h = a * per + u
            state = sin[h]
            mid = dot_ff(xh[h * 2, :, D:], state) + xh[h * 2, :, :D]
            for hf, s0 in enumerate((state, mid)):
                rows = slice(hf * half * B, (hf + 1) * half * B)
                core[h, rows, :] = (base[h, rows, :] + dot_ef(r[h, rows, :], s0)).astype(BF)
            for s in range(1, group):
                send(h, s).start()
            got[me * heads + h] = core[h, mine, :]

    def keys_step(i, carry):
        a, hf = i // 2, lax.rem(i, 2)

        @pl.when(hf == 0)
        def _():
            arrive(0, a)

        by_keys(a, hf)
        return carry

    lax.fori_loop(0, 2 * kheads, keys_step, 0)

    def values_step(i, carry):
        a, hf = i // 2, lax.rem(i, 2)

        @pl.when(hf == 0)
        def _():
            arrive(1, a)

        by_values(a, hf)

        @pl.when(hf == 1)
        def _():
            whole_map(a)

        @pl.when(((i == 1) & (z <= 1)) | ((i == 3) & ((z == 0) | (z == 2))))
        def _():
            pass_on(jnp.where((i == 3) & (z == 0), 1, 0))

        return carry

    lax.fori_loop(0, 2 * kheads, values_step, 0)

    def queries_step(i, carry):
        a, hf = i // 2, lax.rem(i, 2)

        @pl.when(hf == 0)
        def _():
            arrive(2, a)

        by_queries(a, hf)

        @pl.when(((i == 0) & (z == 1)) | ((i == 1) & (z >= 3)) | ((i == 2) & (z == 2)) | ((i == 3) & (z >= 3)))
        def _():
            pass_on(jnp.where(i == 1, 0, 1))

        @pl.when(hf == 1)
        def _():
            finish(a)

        return carry

    lax.fori_loop(0, 2 * kheads, queries_step, 0)
    gate_copy.wait()
    scale = gain[...]

    def norm(i):
        x = got[i].astype(F32)
        cols = pl.ds(pl.multiple_of(i * D, D), D)
        g = gate[:, cols].astype(F32)
        y = x * lax.rsqrt(jnp.mean(x * x, axis=-1, keepdims=True) + 1e-6)
        out[:, cols] = (y * scale * (g / (1.0 + jnp.exp(-g)))).astype(BF)

    def close(h, carry):
        norm(me * heads + h)
        for s in range(1, group):
            send(h, s).wait_recv()
            norm(lax.rem(me + group - s, group) * heads + h)
        return carry

    lax.fori_loop(0, heads, close, 0)

    def drain(a, carry):
        for i in range(3):
            for s in range(1, group):
                large_copy(i, a, s).wait_send()
        for u in range(per):
            h = a * per + u
            for s in range(1, group):
                send(h, s).wait_send()

            @pl.when(z < zs - 1)
            def _():
                chain(h).wait_send()

        return carry

    lax.fori_loop(0, kheads, drain, 0)
    for i in range(2):
        for s in range(1, group):
            small_copy(i, s).wait_send()


def solution(mesh):
    n, m = mesh.shape["head"], mesh.shape["ctx"]
    pair = 2

    def local(q, k, v, gate, be, de, gain):
        t, width = v.shape
        group = n * pair
        heads = width // D // group
        kheads = k.shape[1] // D // group
        per = heads // kheads
        assert kheads == 2
        blocks = t * group // B
        elems = heads * blocks
        vm = pl.BlockSpec(memory_space=pltpu.VMEM)
        hbm = pl.BlockSpec(memory_space=pl.ANY)
        dma = pltpu.SemaphoreType.DMA
        return pl.pallas_call(
            functools.partial(fused_kernel, n, m, pair, kheads, per),
            out_shape=jax.ShapeDtypeStruct((t, width), BF),
            in_specs=[hbm] * 6 + [vm],
            out_specs=vm,
            scratch_shapes=[
                pltpu.VMEM((kheads, t * group, D), BF),
                pltpu.VMEM((kheads, t * group, D), BF),
                pltpu.VMEM((kheads, t * group, per * D), BF),
                pltpu.VMEM((group, be.shape[1], t), BF),
                pltpu.VMEM((group, de.shape[1], t), BF),
                pltpu.VMEM((t, width), BF),
                pltpu.VMEM((elems, B, 2 * B), BF),
                pltpu.VMEM((elems, B, 2 * D), F32),
                pltpu.VMEM((elems, B, B), F32),
                pltpu.VMEM((elems, D, D), BF),
                pltpu.VMEM((elems, D, D), BF),
                pltpu.VMEM((kheads * blocks, D, B), BF),
                pltpu.VMEM((kheads * blocks, B, 8), F32),
                pltpu.VMEM((kheads * blocks, B, 8), F32),
                pltpu.VMEM((elems, 2 * D, 2 * D), BF),
                pltpu.VMEM((heads * 2, D, 2 * D), F32),
                pltpu.VMEM((heads, D, 2 * D), F32),
                pltpu.VMEM((heads, t * group, D), F32),
                pltpu.VMEM((heads, t * group, D), BF),
                pltpu.VMEM((heads, D, D), F32),
                pltpu.VMEM((heads, D, D), F32),
                pltpu.VMEM((heads, t * group, D), BF),
                pltpu.VMEM((heads * group, t, D), BF),
                dma((3, kheads, group)),
                dma((3, kheads, group)),
                dma((3, kheads)),
                dma((2, group)),
                dma((2, group)),
                dma((2,)),
                dma,
                dma((heads,)),
                dma((heads,)),
                dma((heads, group)),
                dma((heads, group)),
            ],
            compiler_params=pltpu.CompilerParams(
                collective_id=0, has_side_effects=True, vmem_limit_bytes=56 << 20
            ),
        )(q, k, v, be.T, de.T, gate, gain.reshape(1, D))

    rows = P(("ctx", "head"), None)
    return jax.shard_map(
        local, mesh=mesh, in_specs=(rows,) * 6 + (P(),), out_specs=rows, check_vma=False
    )
```

```python
import functools

import jax
import jax.numpy as jnp
from jax import lax
from jax.experimental import pallas as pl
from jax.experimental.pallas import tpu as pltpu
from jax.sharding import PartitionSpec as P

D = 128
B = 128
F32 = jnp.float32
BF = jnp.bfloat16
MESH = pl.DeviceIdType.MESH


def split(x):
    hi = x.astype(BF)
    return hi, (x - hi.astype(F32)).astype(BF)


def dot(a, b):
    return jnp.dot(a, b, preferred_element_type=F32)


def dot_t(a, b):
    return lax.dot_general(a, b, (((1,), (1,)), ((), ())), preferred_element_type=F32)


def dot_b(a, b):
    return dot(a.astype(BF), b.astype(BF))


def dot_fe(a, b):
    hi, lo = split(a)
    return dot(jnp.concatenate([hi, lo], 1), jnp.concatenate([b, b], 0))


def dot_ef(a, b):
    hi, lo = split(b)
    return dot(jnp.concatenate([a, a], 1), jnp.concatenate([hi, lo], 0))


def dot_sf(ah, al, b):
    bh, bl = split(b)
    return dot(jnp.concatenate([ah, ah], 1), jnp.concatenate([bh, bl], 0)) + dot(al, bh)


def dot_ff(a, b):
    return dot_sf(*split(a), b)


def odd_rows(x, w):
    return jnp.concatenate([x[i : i + w] for i in range(w, B, 2 * w)], 0)


def weave(even, odd, w):
    parts = []
    for i in range(0, B // 2, w):
        parts += [even[i : i + w], odd[i : i + w]]
    return jnp.concatenate(parts, 0)


def even_rows(x, w):
    return jnp.concatenate([x[i : i + w] for i in range(0, B, 2 * w)], 0)


def unit_lower_inverse(lows, ii, jj):
    eye = (ii == jj).astype(F32)
    base = (ii >> 4) == (jj >> 4)
    p = [jnp.where(base, -x, 0.0) for x in lows]
    pb = [x.astype(BF) for x in p]
    p2 = [dot(x, x) for x in pb]
    p2b = [x.astype(BF) for x in p2]
    z = [dot(x, jnp.concatenate([x, y], 1)) for x, y in zip(p2b, pb)]
    t = [eye + x + y + w[:, B:] for x, y, w in zip(p, p2, z)]
    p4b = [w[:, :B].astype(BF) for w in z]
    z = [dot(x, jnp.concatenate([x, y.astype(BF)], 1)) for x, y in zip(p4b, t)]
    t = [y + w[:, B:] for y, w in zip(t, z)]
    t = [y + dot(w[:, :B].astype(BF), y.astype(BF)) for y, w in zip(t, z)]
    w, bit = 16, 4
    zero = jnp.zeros((B // 2, B), BF)
    while w < B:
        below = odd_rows((ii >> bit) == (jj >> bit) + 1, w)
        tb = [y.astype(BF) for y in t]
        lo = [jnp.where(below, odd_rows(x, w), 0.0).astype(BF) for x in lows]
        z = [dot(x, y).astype(BF) for x, y in zip(lo, tb)]
        d = [dot(odd_rows(y, w), weave(zero, x, w)) for y, x in zip(tb, z)]
        t = [weave(even_rows(y, w), odd_rows(y, w) - x, w) for y, x in zip(t, d)]
        w, bit = 2 * w, bit + 1
    return t


def fused_kernel(
    n, m, pair, kheads, per,
    q, k, v, be, de, gate_hbm, gain,
    out,
    qb, kb, vb, beb, deb, gate, gated, ivs, uw, wr, th, tl, ktb, gates, xsb, xh, xf, base, r, sin, sout, core, got,
    es, er, el, fs, fr, fl, gs, cs, cr, ss, rs,
):
    hx = lax.axis_index("head")
    c = lax.axis_index("ctx")
    group = n * pair
    z = c // pair
    me = lax.rem(c, pair) * n + hx
    zs = m // pair
    heads = kheads * per
    t = q.shape[0]
    wide = beb.shape[1]
    blocks = t * group // B
    half = blocks // 2

    def peer(s):
        rank = lax.rem(me + s, group)
        return {"ctx": z * pair + rank // n, "head": lax.rem(rank, n)}, rank

    barrier = pltpu.get_barrier_semaphore()
    for s in range(1, group):
        pl.semaphore_signal(barrier, inc=1, device_id=peer(s)[0], device_id_type=MESH)
    for s in (pair, m - pair):
        pl.semaphore_signal(barrier, inc=1, device_id={"ctx": lax.rem(c + s, m)}, device_id_type=MESH)
    pl.semaphore_wait(barrier, group + 1)

    mine = pl.ds(pl.multiple_of(me * t, t), t)
    small = ((de, deb), (be, beb))
    large = ((k, kb, D), (v, vb, per * D), (q, qb, D))

    def gates_of(i, rank):
        return small[i][0].at[pl.ds(pl.multiple_of(rank * heads // wide * wide, wide), wide), :]

    def small_copy(i, s):
        device, dest = peer(s)
        return pltpu.make_async_remote_copy(
            src_ref=gates_of(i, dest),
            dst_ref=small[i][1].at[me],
            send_sem=fs.at[i, s],
            recv_sem=fr.at[i, s],
            device_id=device,
            device_id_type=MESH,
        )

    def small_local(i):
        return pltpu.make_async_copy(gates_of(i, me), small[i][1].at[me], fl.at[i])

    def piece(i, a, dest):
        w = large[i][2]
        return large[i][0].at[:, pl.ds(pl.multiple_of((dest * kheads + a) * w, w), w)]

    def large_copy(i, a, s):
        device, dest = peer(s)
        return pltpu.make_async_remote_copy(
            src_ref=piece(i, a, dest),
            dst_ref=large[i][1].at[a, mine, :],
            send_sem=es.at[i, a, s],
            recv_sem=er.at[i, a, s],
            device_id=device,
            device_id_type=MESH,
        )

    def large_local(i, a):
        return pltpu.make_async_copy(piece(i, a, me), large[i][1].at[a, mine, :], el.at[i, a])

    def arrive(i, a):
        for s in range(1, group):
            large_copy(i, a, s).wait_recv()
        large_local(i, a).wait()

    gate_copy = pltpu.make_async_copy(gate_hbm, gate, gs)
    for i in range(2):
        small_local(i).start()
    for a in range(kheads):
        large_local(0, a).start()
    first = [n] + [s for s in range(1, group) if s != n]
    for i in range(2):
        for s in first:
            small_copy(i, s).start()
    for i in range(3):
        for a in range(kheads):
            for s in first:
                large_copy(i, a, s).start()
        if i == 0:
            gate_copy.start()
        else:
            for a in range(kheads):
                large_local(i, a).start()

    ii = lax.broadcasted_iota(jnp.int32, (B, B), 0)
    jj = lax.broadcasted_iota(jnp.int32, (B, B), 1)
    eye = ii == jj
    causal = ii >= jj
    strict = ii > jj
    upp = (ii <= jj).astype(BF)

    def block_rows(blk):
        return pl.ds(pl.multiple_of(blk * B, B), B)

    def by_keys(items):
        first = lax.rem(me * heads, wide)
        idx = [a * blocks + blk for a, blk in items]
        drows, berows = [], []
        for a, blk in items:
            sel_t = (
                lax.broadcasted_iota(jnp.int32, (8, wide), 1)
                == lax.broadcasted_iota(jnp.int32, (8, wide), 0) + (first + a * per)
            ).astype(BF)
            drows.append(dot(sel_t, deb[blk]).astype(BF))
            berows.append(dot(sel_t, beb[blk]))
        kks = [kb[a, block_rows(blk), :] for a, blk in items]
        brows = [dot(x, upp) for x in drows]
        gs_ = [dot_t(x, x) for x in kks]
        kts = [jnp.transpose(x) for x in kks]
        rrs = [lax.rsqrt(jnp.sum(jnp.where(eye, x, 0.0), axis=0, keepdims=True) + 1e-6) for x in gs_]
        grs = [jnp.exp(x) for x in brows]
        turned = []
        for brow, grow, berow, rr in zip(brows, grs, berows, rrs):
            turned.append(jnp.concatenate([brow, jnp.exp(brow[:, B - 1 :] - brow) * rr, berow * rr, grow], 0))
        cols = []
        for i in range(0, len(items), 4):
            some = turned[i : i + 4]
            some += [some[-1]] * (4 - len(some))
            flat = jnp.transpose(jnp.concatenate(some, 0))
            cols += [flat[:, j * 32 : (j + 1) * 32] for j in range(4)]
        lows = []
        for x, col, kt, g, rr, brow in zip(idx, cols, kts, gs_, rrs, brows):
            ktb[x] = kt
            gates[x] = col
            gr = g * rr
            for u in range(per):
                gap = col[:, u : u + 1] - brow[u : u + 1, :]
                wts = jnp.where(causal, jnp.exp(jnp.minimum(gap, 0.0)), 0.0)
                lows.append(jnp.where(strict, col[:, 16 + u : 17 + u] * wts * gr, 0.0))
                wr[x * per + u] = wts * rr
        inv = unit_lower_inverse(lows, ii, jj)
        ws = []
        for i, (x, kk, berow, grow, rr) in enumerate(zip(idx, kks, berows, grs, rrs)):
            bgr = berow * grow * rr
            for u in range(per):
                y = inv[i * per + u]
                ivs[x * per + u] = jnp.concatenate(split(y * berow[u : u + 1, :]), 1)
                ws.append(dot_fe(y * bgr[u : u + 1, :], kk))
        downs = []
        for i, (x, kt, col) in enumerate(zip(idx, kts, cols)):
            ends = []
            for u in range(per):
                w = ws[i * per + u]
                uw[x * per + u, :, D:] = w
                ends.append(col[:, 8 + u : 9 + u] * w)
            downs.append(dot_ef(kt, jnp.concatenate(ends, 1)))
        for x, down, grow in zip(idx, downs, grs):
            for u in range(per):
                trans = jnp.where(eye, grow[u : u + 1, B - 1 :], 0.0) - down[:, u * D : (u + 1) * D]
                th[x * per + u], tl[x * per + u] = split(trans)

    zero = jnp.zeros((B, D), F32)

    def by_values(a):
        freshes = []
        for blk in range(blocks):
            for u in range(per):
                vv = vb[a, blk * B : (blk + 1) * B, u * D : (u + 1) * D]
                freshes.append(dot(ivs[(a * blocks + blk) * per + u], jnp.concatenate([vv, vv], 0)))
        writtens = []
        for blk in range(blocks):
            x = a * blocks + blk
            ends = []
            for u in range(per):
                fresh = freshes[blk * per + u]
                uw[x * per + u, :, :D] = fresh
                ends.append(gates[x, :, 8 + u : 9 + u] * fresh)
            writtens.append(dot_ef(ktb[x], jnp.concatenate(ends, 1)))
        xs = {}
        for b in range(half):
            now = {}
            for hf in range(2):
                blk = hf * half + b
                for u in range(per):
                    e = (a * blocks + blk) * per + u
                    wu = writtens[blk][:, u * D : (u + 1) * D]
                    if b == 0:
                        now[hf, u] = jnp.concatenate([wu, th[e].astype(F32) + tl[e].astype(F32)], 1)
                    else:
                        now[hf, u] = dot_sf(th[e], tl[e], xs[hf, u]) + jnp.concatenate([wu, zero], 1)
                    if b < half - 1:
                        xsb[e] = jnp.concatenate(split(now[hf, u]), 0)
            xs = now
        for u in range(per):
            h = a * per + u
            for hf in range(2):
                xh[h * 2 + hf] = xs[hf, u]
            late = xs[1, u]
            xf[h] = dot_ff(late[:, D:], xs[0, u]) + jnp.concatenate([late[:, :D], zero], 1)

    def by_queries(a):
        hns, qns = [], []
        for blk in range(blocks):
            qq = qb[a, blk * B : (blk + 1) * B, :]
            qf = qq.astype(F32)
            qc = lax.rsqrt(jnp.sum(qf * qf, axis=1, keepdims=True) + 1e-6)
            hns.append(dot_t(qq, kb[a, blk * B : (blk + 1) * B, :]) * qc)
            qns.append(qf * qc)
        todo = []
        for blk in range(blocks):
            x = a * blocks + blk
            for u in range(per):
                e = x * per + u
                lr = dot_ef((wr[e] * hns[blk]).astype(BF), uw[e])
                far = (gates[x, :, 24 + u : 25 + u] * qns[blk] - lr[:, D:]).astype(BF)
                todo.append((blk, u, e, lr[:, :D], far))
        for blk, u, e, near, far in todo:
            if blk % half:
                o = dot(jnp.concatenate([far, far], 1), xsb[e - per])
                near = near + o[:, :D]
                far = o[:, D:].astype(BF)
            base[a * per + u, blk * B : (blk + 1) * B, :] = near
            r[a * per + u, blk * B : (blk + 1) * B, :] = far

    def chain(h):
        return pltpu.make_async_remote_copy(
            src_ref=sout.at[h],
            dst_ref=sin.at[h],
            send_sem=cs.at[h],
            recv_sem=cr.at[h],
            device_id={"ctx": lax.rem(c + pair, m)},
            device_id_type=MESH,
        )

    def send(h, s):
        device, dest = peer(s)
        return pltpu.make_async_remote_copy(
            src_ref=core.at[h, pl.ds(pl.multiple_of(dest * t, t), t), :],
            dst_ref=got.at[me * heads + h],
            send_sem=ss.at[h, s],
            recv_sem=rs.at[h, s],
            device_id=device,
            device_id_type=MESH,
        )

    def pass_on(a):
        for u in range(per):
            h = a * per + u

            @pl.when(z == 0)
            def _():
                sin[h] = jnp.zeros((D, D), F32)
                sout[h] = xf[h, :, :D]

            @pl.when(z > 0)
            def _():
                chain(h).wait_recv()

                @pl.when(z < zs - 1)
                def _():
                    sout[h] = dot_ff(xf[h, :, D:], sin[h]) + xf[h, :, :D]

            @pl.when(z < zs - 1)
            def _():
                chain(h).start()

    def finish(a):
        hs = [a * per + u for u in range(per)]
        mids = [dot_ff(xh[h * 2, :, D:], sin[h]) + xh[h * 2, :, :D] for h in hs]
        for h, mid in zip(hs, mids):
            for hf, s0 in enumerate((sin[h], mid)):
                rows = slice(hf * half * B, (hf + 1) * half * B)
                core[h, rows, :] = (base[h, rows, :] + dot_ef(r[h, rows, :], s0)).astype(BF)
            for s in range(1, group):
                send(h, s).start()

    scale = gain[...]
    gate_copy.wait()

    def gate_step(i, carry):
        cols = pl.ds(pl.multiple_of(i * D, D), D)
        g = gate[:, cols].astype(F32)
        gated[:, cols] = scale * (g / (1.0 + jnp.exp(-g)))
        return carry

    lax.fori_loop(0, heads * group, gate_step, 0)
    for i in range(2):
        small_local(i).wait()
        small_copy(i, n).wait_recv()
    for a in range(kheads):
        large_local(0, a).wait()
        large_copy(0, a, n).wait_recv()
    by_keys([(a, lax.rem(me + s, group)) for a in range(kheads) for s in (0, n)])
    others = [s for s in range(1, group) if s != n]
    for i in range(2):
        for s in others:
            small_copy(i, s).wait_recv()

    def keys_step(a, carry):
        for s in others:
            large_copy(0, a, s).wait_recv()
        by_keys([(a, lax.rem(me + s, group)) for s in others])
        return carry

    lax.fori_loop(0, kheads, keys_step, 0)

    def values_step(a, carry):
        arrive(1, a)
        by_values(a)

        @pl.when(jnp.where(a == 0, z <= 1, (z == 0) | (z == 2)))
        def _():
            pass_on(jnp.where((a == 1) & (z == 0), 1, 0))

        return carry

    lax.fori_loop(0, kheads, values_step, 0)

    def queries_step(a, carry):
        @pl.when((a == 0) & (z == 1))
        def _():
            pass_on(1)

        arrive(2, a)
        by_queries(a)

        @pl.when(jnp.where(a == 0, z >= 3, z >= 2))
        def _():
            pass_on(a)

        finish(a)
        return carry

    lax.fori_loop(0, kheads, queries_step, 0)

    def norm(i, x):
        x = x.astype(F32)
        cols = pl.ds(pl.multiple_of(i * D, D), D)
        y = x * lax.rsqrt(jnp.mean(x * x, axis=-1, keepdims=True) + 1e-6)
        out[:, cols] = (y * gated[:, cols]).astype(BF)

    def close(h, carry):
        norm(me * heads + h, core[h, mine, :])
        for s in range(1, group):
            send(h, s).wait_recv()
            i = lax.rem(me + group - s, group) * heads + h
            norm(i, got[i])
        return carry

    lax.fori_loop(0, heads, close, 0)

    def drain(a, carry):
        for i in range(3):
            for s in range(1, group):
                large_copy(i, a, s).wait_send()
        for u in range(per):
            h = a * per + u
            for s in range(1, group):
                send(h, s).wait_send()

            @pl.when(z < zs - 1)
            def _():
                chain(h).wait_send()

        return carry

    lax.fori_loop(0, kheads, drain, 0)
    for i in range(2):
        for s in range(1, group):
            small_copy(i, s).wait_send()


def solution(mesh):
    n, m = mesh.shape["head"], mesh.shape["ctx"]
    pair = 2

    def local(q, k, v, gate, be, de, gain):
        t, width = v.shape
        group = n * pair
        heads = width // D // group
        kheads = k.shape[1] // D // group
        per = heads // kheads
        blocks = t * group // B
        wide = 16
        assert kheads == per == 2 and blocks == group and wide % heads == 0
        elems = heads * blocks
        vm = pl.BlockSpec(memory_space=pltpu.VMEM)
        hbm = pl.BlockSpec(memory_space=pl.ANY)
        dma = pltpu.SemaphoreType.DMA
        return pl.pallas_call(
            functools.partial(fused_kernel, n, m, pair, kheads, per),
            out_shape=jax.ShapeDtypeStruct((t, width), BF),
            in_specs=[hbm] * 6 + [vm],
            out_specs=vm,
            scratch_shapes=[
                pltpu.VMEM((kheads, t * group, D), BF),
                pltpu.VMEM((kheads, t * group, D), BF),
                pltpu.VMEM((kheads, t * group, per * D), BF),
                pltpu.VMEM((group, wide, t), BF),
                pltpu.VMEM((group, wide, t), BF),
                pltpu.VMEM((t, width), BF),
                pltpu.VMEM((t, width), F32),
                pltpu.VMEM((elems, B, 2 * B), BF),
                pltpu.VMEM((elems, B, 2 * D), F32),
                pltpu.VMEM((elems, B, B), F32),
                pltpu.VMEM((elems, D, D), BF),
                pltpu.VMEM((elems, D, D), BF),
                pltpu.VMEM((kheads * blocks, D, B), BF),
                pltpu.VMEM((kheads * blocks, B, 32), F32),
                pltpu.VMEM((elems, 2 * D, 2 * D), BF),
                pltpu.VMEM((heads * 2, D, 2 * D), F32),
                pltpu.VMEM((heads, D, 2 * D), F32),
                pltpu.VMEM((heads, t * group, D), F32),
                pltpu.VMEM((heads, t * group, D), BF),
                pltpu.VMEM((heads, D, D), F32),
                pltpu.VMEM((heads, D, D), F32),
                pltpu.VMEM((heads, t * group, D), BF),
                pltpu.VMEM((heads * group, t, D), BF),
                dma((3, kheads, group)),
                dma((3, kheads, group)),
                dma((3, kheads)),
                dma((2, group)),
                dma((2, group)),
                dma((2,)),
                dma,
                dma((heads,)),
                dma((heads,)),
                dma((heads, group)),
                dma((heads, group)),
            ],
            compiler_params=pltpu.CompilerParams(
                collective_id=0, has_side_effects=True, vmem_limit_bytes=56 << 20
            ),
        )(q, k, v, be.T, de.T, gate, gain.reshape(1, D))

    rows = P(("ctx", "head"), None)
    return jax.shard_map(
        local, mesh=mesh, in_specs=(rows,) * 6 + (P(),), out_specs=rows, check_vma=False
    )
```

```python
import functools

import jax
import jax.numpy as jnp
from jax import lax
from jax.experimental import pallas as pl
from jax.experimental.pallas import tpu as pltpu
from jax.sharding import PartitionSpec as P

D = 128
B = 128
F32 = jnp.float32
BF = jnp.bfloat16
MESH = pl.DeviceIdType.MESH


def split(x):
    hi = x.astype(BF)
    return hi, (x - hi.astype(F32)).astype(BF)


def dot(a, b):
    return jnp.dot(a, b, preferred_element_type=F32)


def dot_t(a, b):
    return lax.dot_general(a, b, (((1,), (1,)), ((), ())), preferred_element_type=F32)


def dot_b(a, b):
    return dot(a.astype(BF), b.astype(BF))


def dot_fe(a, b):
    hi, lo = split(a)
    return dot(jnp.concatenate([hi, lo], 1), jnp.concatenate([b, b], 0))


def dot_ef(a, b):
    hi, lo = split(b)
    return dot(jnp.concatenate([a, a], 1), jnp.concatenate([hi, lo], 0))


def dot_sf(ah, al, b):
    bh, bl = split(b)
    return dot(jnp.concatenate([ah, ah], 1), jnp.concatenate([bh, bl], 0)) + dot(al, bh)


def dot_ff(a, b):
    return dot_sf(*split(a), b)


def odd_rows(x, w):
    return jnp.concatenate([x[i : i + w] for i in range(w, B, 2 * w)], 0)


def weave(even, odd, w):
    parts = []
    for i in range(0, B // 2, w):
        parts += [even[i : i + w], odd[i : i + w]]
    return jnp.concatenate(parts, 0)


def even_rows(x, w):
    return jnp.concatenate([x[i : i + w] for i in range(0, B, 2 * w)], 0)


def unit_lower_inverse(lows, ii, jj):
    eye = (ii == jj).astype(F32)
    base = (ii >> 4) == (jj >> 4)
    p = [jnp.where(base, -x, 0.0) for x in lows]
    pb = [x.astype(BF) for x in p]
    p2 = [dot(x, x) for x in pb]
    p2b = [x.astype(BF) for x in p2]
    z = [dot(x, jnp.concatenate([x, y], 1)) for x, y in zip(p2b, pb)]
    t = [eye + x + y + w[:, B:] for x, y, w in zip(p, p2, z)]
    p4b = [w[:, :B].astype(BF) for w in z]
    z = [dot(x, jnp.concatenate([x, y.astype(BF)], 1)) for x, y in zip(p4b, t)]
    t = [y + w[:, B:] for y, w in zip(t, z)]
    t = [y + dot(w[:, :B].astype(BF), y.astype(BF)) for y, w in zip(t, z)]
    w, bit = 16, 4
    zero = jnp.zeros((B // 2, B), BF)
    while w < B:
        below = odd_rows((ii >> bit) == (jj >> bit) + 1, w)
        tb = [y.astype(BF) for y in t]
        lo = [jnp.where(below, odd_rows(x, w), 0.0).astype(BF) for x in lows]
        z = [dot(x, y).astype(BF) for x, y in zip(lo, tb)]
        d = [dot(odd_rows(y, w), weave(zero, x, w)) for y, x in zip(tb, z)]
        t = [weave(even_rows(y, w), odd_rows(y, w) - x, w) for y, x in zip(t, d)]
        w, bit = 2 * w, bit + 1
    return t


def fused_kernel(
    n, m, pair, kheads, per,
    q, k, v, be, de, gate_hbm, gain,
    out,
    qb, kb, vb, beb, deb, gate, gated, ivs, uw, wr, th, tl, ktb, gates, xsb, xh, xf, base, r, sin, sout, core, got,
    es, er, el, fs, fr, fl, gs, cs, cr, ss, rs,
):
    hx = lax.axis_index("head")
    c = lax.axis_index("ctx")
    group = n * pair
    z = c // pair
    me = lax.rem(c, pair) * n + hx
    zs = m // pair
    heads = kheads * per
    t = q.shape[0]
    wide = beb.shape[1]
    blocks = t * group // B
    half = blocks // 2

    def peer(s):
        rank = lax.rem(me + s, group)
        return {"ctx": z * pair + rank // n, "head": lax.rem(rank, n)}, rank

    barrier = pltpu.get_barrier_semaphore()
    for s in range(1, group):
        pl.semaphore_signal(barrier, inc=1, device_id=peer(s)[0], device_id_type=MESH)
    for s in (pair, m - pair):
        pl.semaphore_signal(barrier, inc=1, device_id={"ctx": lax.rem(c + s, m)}, device_id_type=MESH)
    pl.semaphore_wait(barrier, group + 1)

    mine = pl.ds(pl.multiple_of(me * t, t), t)
    small = ((de, deb), (be, beb))
    large = ((k, kb, D), (v, vb, per * D), (q, qb, D))

    def gates_of(i, rank):
        return small[i][0].at[pl.ds(pl.multiple_of(rank * heads // wide * wide, wide), wide), :]

    def small_copy(i, s):
        device, dest = peer(s)
        return pltpu.make_async_remote_copy(
            src_ref=gates_of(i, dest),
            dst_ref=small[i][1].at[me],
            send_sem=fs.at[i, s],
            recv_sem=fr.at[i, s],
            device_id=device,
            device_id_type=MESH,
        )

    def small_local(i):
        return pltpu.make_async_copy(gates_of(i, me), small[i][1].at[me], fl.at[i])

    def piece(i, a, dest):
        w = large[i][2]
        return large[i][0].at[:, pl.ds(pl.multiple_of((dest * kheads + a) * w, w), w)]

    def large_copy(i, a, s):
        device, dest = peer(s)
        return pltpu.make_async_remote_copy(
            src_ref=piece(i, a, dest),
            dst_ref=large[i][1].at[a, mine, :],
            send_sem=es.at[i, a, s],
            recv_sem=er.at[i, a, s],
            device_id=device,
            device_id_type=MESH,
        )

    def large_local(i, a):
        return pltpu.make_async_copy(piece(i, a, me), large[i][1].at[a, mine, :], el.at[i, a])

    def arrive(i, a):
        for s in range(1, group):
            large_copy(i, a, s).wait_recv()
        large_local(i, a).wait()

    gate_copy = pltpu.make_async_copy(gate_hbm, gate, gs)
    for i in range(2):
        small_local(i).start()
    for a in range(kheads):
        large_local(0, a).start()
    first = [n] + [s for s in range(1, group) if s != n]
    for i in range(2):
        for s in first:
            small_copy(i, s).start()
    for i in range(3):
        for a in range(kheads):
            for s in first:
                large_copy(i, a, s).start()
        if i == 0:
            gate_copy.start()
        else:
            for a in range(kheads):
                large_local(i, a).start()

    ii = lax.broadcasted_iota(jnp.int32, (B, B), 0)
    jj = lax.broadcasted_iota(jnp.int32, (B, B), 1)
    eye = ii == jj
    causal = ii >= jj
    strict = ii > jj
    upp = (ii <= jj).astype(BF)

    def block_rows(blk):
        return pl.ds(pl.multiple_of(blk * B, B), B)

    def by_keys(items):
        first = lax.rem(me * heads, wide)
        idx = [a * blocks + blk for a, blk in items]
        drows, berows = [], []
        for a, blk in items:
            sel_t = (
                lax.broadcasted_iota(jnp.int32, (8, wide), 1)
                == lax.broadcasted_iota(jnp.int32, (8, wide), 0) + (first + a * per)
            ).astype(BF)
            drows.append(dot(sel_t, deb[blk]).astype(BF))
            berows.append(dot(sel_t, beb[blk]))
        kks = [kb[a, block_rows(blk), :] for a, blk in items]
        brows = [dot(x, upp) for x in drows]
        gs_ = [dot_t(x, x) for x in kks]
        kts = [jnp.transpose(x) for x in kks]
        rrs = [lax.rsqrt(jnp.sum(jnp.where(eye, x, 0.0), axis=0, keepdims=True) + 1e-6) for x in gs_]
        grs = [jnp.exp(x) for x in brows]
        turned = []
        for brow, grow, berow, rr in zip(brows, grs, berows, rrs):
            turned.append(jnp.concatenate([brow, jnp.exp(brow[:, B - 1 :] - brow) * rr, berow * rr, grow], 0))
        cols = []
        for i in range(0, len(items), 4):
            some = turned[i : i + 4]
            some += [some[-1]] * (4 - len(some))
            flat = jnp.transpose(jnp.concatenate(some, 0))
            cols += [flat[:, j * 32 : (j + 1) * 32] for j in range(4)]
        lows = []
        for x, col, kt, g, rr, brow in zip(idx, cols, kts, gs_, rrs, brows):
            ktb[x] = kt
            gates[x] = col
            gr = g * rr
            for u in range(per):
                gap = col[:, u : u + 1] - brow[u : u + 1, :]
                wts = jnp.where(causal, jnp.exp(jnp.minimum(gap, 0.0)), 0.0)
                lows.append(jnp.where(strict, col[:, 16 + u : 17 + u] * wts * gr, 0.0))
                wr[x * per + u] = wts * rr
        inv = unit_lower_inverse(lows, ii, jj)
        ws = []
        for i, (x, kk, berow, grow, rr) in enumerate(zip(idx, kks, berows, grs, rrs)):
            bgr = berow * grow * rr
            for u in range(per):
                y = inv[i * per + u]
                ivs[x * per + u] = jnp.concatenate(split(y * berow[u : u + 1, :]), 1)
                ws.append(dot_fe(y * bgr[u : u + 1, :], kk))
        downs = []
        for i, (x, kt, col) in enumerate(zip(idx, kts, cols)):
            ends = []
            for u in range(per):
                w = ws[i * per + u]
                uw[x * per + u, :, D:] = w
                ends.append(col[:, 8 + u : 9 + u] * w)
            downs.append(dot_ef(kt, jnp.concatenate(ends, 1)))
        for x, down, grow in zip(idx, downs, grs):
            for u in range(per):
                trans = jnp.where(eye, grow[u : u + 1, B - 1 :], 0.0) - down[:, u * D : (u + 1) * D]
                th[x * per + u], tl[x * per + u] = split(trans)

    zero = jnp.zeros((B, D), F32)

    def by_values(a):
        freshes = []
        for blk in range(blocks):
            for u in range(per):
                vv = vb[a, blk * B : (blk + 1) * B, u * D : (u + 1) * D]
                freshes.append(dot(ivs[(a * blocks + blk) * per + u], jnp.concatenate([vv, vv], 0)))
        writtens = []
        for blk in range(blocks):
            x = a * blocks + blk
            ends = []
            for u in range(per):
                fresh = freshes[blk * per + u]
                uw[x * per + u, :, :D] = fresh
                ends.append(gates[x, :, 8 + u : 9 + u] * fresh)
            writtens.append(dot_ef(ktb[x], jnp.concatenate(ends, 1)))
        xs = {}
        for b in range(half):
            now = {}
            for hf in range(2):
                blk = hf * half + b
                for u in range(per):
                    e = (a * blocks + blk) * per + u
                    wu = writtens[blk][:, u * D : (u + 1) * D]
                    if b == 0:
                        now[hf, u] = jnp.concatenate([wu, th[e].astype(F32) + tl[e].astype(F32)], 1)
                    else:
                        now[hf, u] = dot_sf(th[e], tl[e], xs[hf, u]) + jnp.concatenate([wu, zero], 1)
                    if b < half - 1:
                        xsb[e] = jnp.concatenate(split(now[hf, u]), 0)
            xs = now
        for u in range(per):
            h = a * per + u
            for hf in range(2):
                xh[h * 2 + hf] = xs[hf, u]
            late = xs[1, u]
            xf[h] = dot_ff(late[:, D:], xs[0, u]) + jnp.concatenate([late[:, :D], zero], 1)

    def by_queries(a):
        hns, qns = [], []
        for blk in range(blocks):
            qq = qb[a, blk * B : (blk + 1) * B, :]
            qf = qq.astype(F32)
            qc = lax.rsqrt(jnp.sum(qf * qf, axis=1, keepdims=True) + 1e-6)
            hns.append(dot_t(qq, kb[a, blk * B : (blk + 1) * B, :]) * qc)
            qns.append(qf * qc)
        todo = []
        for blk in range(blocks):
            x = a * blocks + blk
            for u in range(per):
                e = x * per + u
                lr = dot_ef((wr[e] * hns[blk]).astype(BF), uw[e])
                far = (gates[x, :, 24 + u : 25 + u] * qns[blk] - lr[:, D:]).astype(BF)
                todo.append((blk, u, e, lr[:, :D], far))
        for blk, u, e, near, far in todo:
            if blk % half:
                o = dot(jnp.concatenate([far, far], 1), xsb[e - per])
                near = near + o[:, :D]
                far = o[:, D:].astype(BF)
            base[a * per + u, blk * B : (blk + 1) * B, :] = near
            r[a * per + u, blk * B : (blk + 1) * B, :] = far

    def chain(h):
        return pltpu.make_async_remote_copy(
            src_ref=sout.at[h],
            dst_ref=sin.at[h],
            send_sem=cs.at[h],
            recv_sem=cr.at[h],
            device_id={"ctx": lax.rem(c + pair, m)},
            device_id_type=MESH,
        )

    def send(h, s):
        device, dest = peer(s)
        return pltpu.make_async_remote_copy(
            src_ref=core.at[h, pl.ds(pl.multiple_of(dest * t, t), t), :],
            dst_ref=got.at[me * heads + h],
            send_sem=ss.at[h, s],
            recv_sem=rs.at[h, s],
            device_id=device,
            device_id_type=MESH,
        )

    def pass_on(a):
        for u in range(per):
            h = a * per + u

            @pl.when(z == 0)
            def _():
                sin[h] = jnp.zeros((D, D), F32)
                sout[h] = xf[h, :, :D]

            @pl.when(z > 0)
            def _():
                chain(h).wait_recv()

                @pl.when(z < zs - 1)
                def _():
                    sout[h] = dot_ff(xf[h, :, D:], sin[h]) + xf[h, :, :D]

            @pl.when(z < zs - 1)
            def _():
                chain(h).start()

    def finish(a):
        hs = [a * per + u for u in range(per)]
        mids = [dot_ff(xh[h * 2, :, D:], sin[h]) + xh[h * 2, :, :D] for h in hs]
        for h, mid in zip(hs, mids):
            for hf, s0 in enumerate((sin[h], mid)):
                rows = slice(hf * half * B, (hf + 1) * half * B)
                core[h, rows, :] = (base[h, rows, :] + dot_ef(r[h, rows, :], s0)).astype(BF)
            for s in range(1, group):
                send(h, s).start()

    scale = gain[...]
    gate_copy.wait()

    def gate_step(i, carry):
        cols = pl.ds(pl.multiple_of(i * D, D), D)
        g = gate[:, cols].astype(F32)
        gated[:, cols] = scale * (g / (1.0 + jnp.exp(-g)))
        return carry

    lax.fori_loop(0, heads * group, gate_step, 0)
    for i in range(2):
        small_local(i).wait()
        small_copy(i, n).wait_recv()
    for a in range(kheads):
        large_local(0, a).wait()
        large_copy(0, a, n).wait_recv()
    by_keys([(a, lax.rem(me + s, group)) for a in range(kheads) for s in (0, n)])
    others = [s for s in range(1, group) if s != n]
    for i in range(2):
        for s in others:
            small_copy(i, s).wait_recv()

    def keys_step(a, carry):
        for s in others:
            large_copy(0, a, s).wait_recv()
        by_keys([(a, lax.rem(me + s, group)) for s in others])
        return carry

    lax.fori_loop(0, kheads, keys_step, 0)

    def values_step(a, carry):
        arrive(1, a)
        by_values(a)

        @pl.when(jnp.where(a == 0, z <= 1, (z == 0) | (z == 2)))
        def _():
            pass_on(jnp.where((a == 1) & (z == 0), 1, 0))

        return carry

    lax.fori_loop(0, kheads, values_step, 0)

    def queries_step(a, carry):
        @pl.when((a == 0) & (z == 1))
        def _():
            pass_on(1)

        arrive(2, a)
        by_queries(a)

        @pl.when(jnp.where(a == 0, z >= 3, z >= 2))
        def _():
            pass_on(a)

        finish(a)
        return carry

    lax.fori_loop(0, kheads, queries_step, 0)

    def norm(i, x):
        x = x.astype(F32)
        cols = pl.ds(pl.multiple_of(i * D, D), D)
        y = x * lax.rsqrt(jnp.mean(x * x, axis=-1, keepdims=True) + 1e-6)
        out[:, cols] = (y * gated[:, cols]).astype(BF)

    def close(h, carry):
        norm(me * heads + h, core[h, mine, :])
        for s in range(1, group):
            send(h, s).wait_recv()
            i = lax.rem(me + group - s, group) * heads + h
            norm(i, got[i])
        return carry

    lax.fori_loop(0, heads, close, 0)

    def drain(a, carry):
        for i in range(3):
            for s in range(1, group):
                large_copy(i, a, s).wait_send()
        for u in range(per):
            h = a * per + u
            for s in range(1, group):
                send(h, s).wait_send()

            @pl.when(z < zs - 1)
            def _():
                chain(h).wait_send()

        return carry

    lax.fori_loop(0, kheads, drain, 0)
    for i in range(2):
        for s in range(1, group):
            small_copy(i, s).wait_send()


def solution(mesh):
    n, m = mesh.shape["head"], mesh.shape["ctx"]
    pair = 2

    def local(q, k, v, gate, be, de, gain):
        t, width = v.shape
        group = n * pair
        heads = width // D // group
        kheads = k.shape[1] // D // group
        per = heads // kheads
        blocks = t * group // B
        wide = 16
        assert kheads == per == 2 and blocks == group and wide % heads == 0
        elems = heads * blocks
        vm = pl.BlockSpec(memory_space=pltpu.VMEM)
        hbm = pl.BlockSpec(memory_space=pl.ANY)
        dma = pltpu.SemaphoreType.DMA
        return pl.pallas_call(
            functools.partial(fused_kernel, n, m, pair, kheads, per),
            out_shape=pltpu.VMEM((t, width), BF),
            in_specs=[hbm] * 6 + [vm],
            out_specs=vm,
            scratch_shapes=[
                pltpu.VMEM((kheads, t * group, D), BF),
                pltpu.VMEM((kheads, t * group, D), BF),
                pltpu.VMEM((kheads, t * group, per * D), BF),
                pltpu.VMEM((group, wide, t), BF),
                pltpu.VMEM((group, wide, t), BF),
                pltpu.VMEM((t, width), BF),
                pltpu.VMEM((t, width), F32),
                pltpu.VMEM((elems, B, 2 * B), BF),
                pltpu.VMEM((elems, B, 2 * D), F32),
                pltpu.VMEM((elems, B, B), F32),
                pltpu.VMEM((elems, D, D), BF),
                pltpu.VMEM((elems, D, D), BF),
                pltpu.VMEM((kheads * blocks, D, B), BF),
                pltpu.VMEM((kheads * blocks, B, 32), F32),
                pltpu.VMEM((elems, 2 * D, 2 * D), BF),
                pltpu.VMEM((heads * 2, D, 2 * D), F32),
                pltpu.VMEM((heads, D, 2 * D), F32),
                pltpu.VMEM((heads, t * group, D), F32),
                pltpu.VMEM((heads, t * group, D), BF),
                pltpu.VMEM((heads, D, D), F32),
                pltpu.VMEM((heads, D, D), F32),
                pltpu.VMEM((heads, t * group, D), BF),
                pltpu.VMEM((heads * group, t, D), BF),
                dma((3, kheads, group)),
                dma((3, kheads, group)),
                dma((3, kheads)),
                dma((2, group)),
                dma((2, group)),
                dma((2,)),
                dma,
                dma((heads,)),
                dma((heads,)),
                dma((heads, group)),
                dma((heads, group)),
            ],
            compiler_params=pltpu.CompilerParams(
                collective_id=0, has_side_effects=True, vmem_limit_bytes=56 << 20
            ),
        )(q, k, v, be.T, de.T, gate, gain.reshape(1, D))

    rows = P(("ctx", "head"), None)
    return jax.shard_map(
        local, mesh=mesh, in_specs=(rows,) * 6 + (P(),), out_specs=rows, check_vma=False
    )
```

```python
import functools

import jax
import jax.numpy as jnp
from jax import lax
from jax.experimental import pallas as pl
from jax.experimental.pallas import tpu as pltpu
from jax.sharding import PartitionSpec as P

D = 128
B = 128
F32 = jnp.float32
BF = jnp.bfloat16
MESH = pl.DeviceIdType.MESH


def split(x):
    hi = x.astype(BF)
    return hi, (x - hi.astype(F32)).astype(BF)


def dot(a, b):
    return jnp.dot(a, b, preferred_element_type=F32)


def dot_t(a, b):
    return lax.dot_general(a, b, (((1,), (1,)), ((), ())), preferred_element_type=F32)


def dot_b(a, b):
    return dot(a.astype(BF), b.astype(BF))


def dot_fe(a, b):
    hi, lo = split(a)
    return dot(jnp.concatenate([hi, lo], 1), jnp.concatenate([b, b], 0))


def dot_ef(a, b):
    hi, lo = split(b)
    return dot(jnp.concatenate([a, a], 1), jnp.concatenate([hi, lo], 0))


def dot_sf(ah, al, b):
    bh, bl = split(b)
    return dot(jnp.concatenate([ah, ah], 1), jnp.concatenate([bh, bl], 0)) + dot(al, bh)


def dot_ff(a, b):
    return dot_sf(*split(a), b)


def odd_rows(x, w):
    return jnp.concatenate([x[i : i + w] for i in range(w, B, 2 * w)], 0)


def weave(even, odd, w):
    parts = []
    for i in range(0, B // 2, w):
        parts += [even[i : i + w], odd[i : i + w]]
    return jnp.concatenate(parts, 0)


def even_rows(x, w):
    return jnp.concatenate([x[i : i + w] for i in range(0, B, 2 * w)], 0)


def unit_lower_inverse(lows, ii, jj):
    eye = (ii == jj).astype(F32)
    base = (ii >> 4) == (jj >> 4)
    p = [jnp.where(base, -x, 0.0) for x in lows]
    pb = [x.astype(BF) for x in p]
    p2 = [dot(x, x) for x in pb]
    p2b = [x.astype(BF) for x in p2]
    z = [dot(x, jnp.concatenate([x, y], 1)) for x, y in zip(p2b, pb)]
    t = [eye + x + y + w[:, B:] for x, y, w in zip(p, p2, z)]
    p4b = [w[:, :B].astype(BF) for w in z]
    z = [dot(x, jnp.concatenate([x, y.astype(BF)], 1)) for x, y in zip(p4b, t)]
    t = [y + w[:, B:] for y, w in zip(t, z)]
    t = [y + dot(w[:, :B].astype(BF), y.astype(BF)) for y, w in zip(t, z)]
    w, bit = 16, 4
    zero = jnp.zeros((B // 2, B), BF)
    while w < B:
        below = odd_rows((ii >> bit) == (jj >> bit) + 1, w)
        tb = [y.astype(BF) for y in t]
        lo = [jnp.where(below, odd_rows(x, w), 0.0).astype(BF) for x in lows]
        z = [dot(x, y).astype(BF) for x, y in zip(lo, tb)]
        d = [dot(odd_rows(y, w), weave(zero, x, w)) for y, x in zip(tb, z)]
        t = [weave(even_rows(y, w), odd_rows(y, w) - x, w) for y, x in zip(t, d)]
        w, bit = 2 * w, bit + 1
    return t


def fused_kernel(
    n, m, pair, kheads, per,
    q, k, v, be, de, gate_hbm, gain,
    out,
    qb, kb, vb, beb, deb, gate, gated, ivs, uw, wr, th, tl, ktb, gates, xsb, xh, xf, base, r, sin, sout, core, got,
    es, er, el, fs, fr, fl, gs, cs, cr, ss, rs,
):
    hx = lax.axis_index("head")
    c = lax.axis_index("ctx")
    group = n * pair
    z = c // pair
    me = lax.rem(c, pair) * n + hx
    zs = m // pair
    heads = kheads * per
    t = q.shape[0]
    wide = beb.shape[1]
    blocks = t * group // B
    half = blocks // 2

    def peer(s):
        rank = lax.rem(me + s, group)
        return {"ctx": z * pair + rank // n, "head": lax.rem(rank, n)}, rank

    barrier = pltpu.get_barrier_semaphore()
    for s in range(1, group):
        pl.semaphore_signal(barrier, inc=1, device_id=peer(s)[0], device_id_type=MESH)
    for s in (pair, m - pair):
        pl.semaphore_signal(barrier, inc=1, device_id={"ctx": lax.rem(c + s, m)}, device_id_type=MESH)
    mine = pl.ds(pl.multiple_of(me * t, t), t)
    small = ((de, deb), (be, beb))
    large = ((k, kb, D), (v, vb, per * D), (q, qb, D))

    def gates_of(i, rank):
        return small[i][0].at[pl.ds(pl.multiple_of(rank * heads // wide * wide, wide), wide), :]

    def small_copy(i, s):
        device, dest = peer(s)
        return pltpu.make_async_remote_copy(
            src_ref=gates_of(i, dest),
            dst_ref=small[i][1].at[me],
            send_sem=fs.at[i, s],
            recv_sem=fr.at[i, s],
            device_id=device,
            device_id_type=MESH,
        )

    def small_local(i):
        return pltpu.make_async_copy(gates_of(i, me), small[i][1].at[me], fl.at[i])

    def piece(i, a, dest):
        w = large[i][2]
        return large[i][0].at[:, pl.ds(pl.multiple_of((dest * kheads + a) * w, w), w)]

    def large_copy(i, a, s):
        device, dest = peer(s)
        return pltpu.make_async_remote_copy(
            src_ref=piece(i, a, dest),
            dst_ref=large[i][1].at[a, mine, :],
            send_sem=es.at[i, a, s],
            recv_sem=er.at[i, a, s],
            device_id=device,
            device_id_type=MESH,
        )

    def large_local(i, a):
        return pltpu.make_async_copy(piece(i, a, me), large[i][1].at[a, mine, :], el.at[i, a])

    def arrive(i, a):
        for s in range(1, group):
            large_copy(i, a, s).wait_recv()
        large_local(i, a).wait()

    gate_copy = pltpu.make_async_copy(gate_hbm, gate, gs)
    gate_copy.start()
    for i in range(2):
        small_local(i).start()
    for a in range(kheads):
        large_local(0, a).start()
    pl.semaphore_wait(barrier, group + 1)
    others = [s for s in range(1, group) if s != n]
    for a in range(kheads):
        large_copy(0, a, n).start()
    for i in range(2):
        small_copy(i, n).start()
    for s in others:
        large_copy(0, 0, s).start()
    for i in range(2):
        for s in others:
            small_copy(i, s).start()
    for s in others:
        large_copy(0, 1, s).start()
    for i in (1, 2):
        for a in range(kheads):
            for s in [n] + others:
                large_copy(i, a, s).start()
            large_local(i, a).start()

    ii = lax.broadcasted_iota(jnp.int32, (B, B), 0)
    jj = lax.broadcasted_iota(jnp.int32, (B, B), 1)
    eye = ii == jj
    causal = ii >= jj
    strict = ii > jj
    upp = (ii <= jj).astype(BF)

    def block_rows(blk):
        return pl.ds(pl.multiple_of(blk * B, B), B)

    def by_keys(items):
        first = lax.rem(me * heads, wide)
        idx = [a * blocks + blk for a, blk in items]
        drows, berows = [], []
        for a, blk in items:
            sel_t = (
                lax.broadcasted_iota(jnp.int32, (8, wide), 1)
                == lax.broadcasted_iota(jnp.int32, (8, wide), 0) + (first + a * per)
            ).astype(BF)
            drows.append(dot(sel_t, deb[blk]).astype(BF))
            berows.append(dot(sel_t, beb[blk]))
        kks = [kb[a, block_rows(blk), :] for a, blk in items]
        brows = [dot(x, upp) for x in drows]
        gs_ = [dot_t(x, x) for x in kks]
        kts = [jnp.transpose(x) for x in kks]
        rrs = [lax.rsqrt(jnp.sum(jnp.where(eye, x, 0.0), axis=0, keepdims=True) + 1e-6) for x in gs_]
        grs = [jnp.exp(x) for x in brows]
        turned = []
        for brow, grow, berow, rr in zip(brows, grs, berows, rrs):
            turned.append(jnp.concatenate([brow, jnp.exp(brow[:, B - 1 :] - brow) * rr, berow * rr, grow], 0))
        cols = []
        for i in range(0, len(items), 4):
            some = turned[i : i + 4]
            some += [some[-1]] * (4 - len(some))
            flat = jnp.transpose(jnp.concatenate(some, 0))
            cols += [flat[:, j * 32 : (j + 1) * 32] for j in range(4)]
        lows = []
        for x, col, kt, g, rr, brow in zip(idx, cols, kts, gs_, rrs, brows):
            ktb[x] = kt
            gates[x] = col
            gr = g * rr
            for u in range(per):
                gap = col[:, u : u + 1] - brow[u : u + 1, :]
                wts = jnp.where(causal, jnp.exp(jnp.minimum(gap, 0.0)), 0.0)
                lows.append(jnp.where(strict, col[:, 16 + u : 17 + u] * wts * gr, 0.0))
                wr[x * per + u] = wts * rr
        inv = unit_lower_inverse(lows, ii, jj)
        ws = []
        for i, (x, kk, berow, grow, rr) in enumerate(zip(idx, kks, berows, grs, rrs)):
            bgr = berow * grow * rr
            for u in range(per):
                y = inv[i * per + u]
                ivs[x * per + u] = jnp.concatenate(split(y * berow[u : u + 1, :]), 1)
                ws.append(dot_fe(y * bgr[u : u + 1, :], kk))
        downs = []
        for i, (x, kt, col) in enumerate(zip(idx, kts, cols)):
            ends = []
            for u in range(per):
                w = ws[i * per + u]
                uw[x * per + u, :, D:] = w
                ends.append(col[:, 8 + u : 9 + u] * w)
            downs.append(dot_ef(kt, jnp.concatenate(ends, 1)))
        for x, down, grow in zip(idx, downs, grs):
            for u in range(per):
                trans = jnp.where(eye, grow[u : u + 1, B - 1 :], 0.0) - down[:, u * D : (u + 1) * D]
                th[x * per + u], tl[x * per + u] = split(trans)

    zero = jnp.zeros((B, D), F32)

    def by_values(a):
        freshes = []
        for blk in range(blocks):
            for u in range(per):
                vv = vb[a, blk * B : (blk + 1) * B, u * D : (u + 1) * D]
                freshes.append(dot(ivs[(a * blocks + blk) * per + u], jnp.concatenate([vv, vv], 0)))
        writtens = []
        for blk in range(blocks):
            x = a * blocks + blk
            ends = []
            for u in range(per):
                fresh = freshes[blk * per + u]
                uw[x * per + u, :, :D] = fresh
                ends.append(gates[x, :, 8 + u : 9 + u] * fresh)
            writtens.append(dot_ef(ktb[x], jnp.concatenate(ends, 1)))
        xs = {}
        for b in range(half):
            now = {}
            for hf in range(2):
                blk = hf * half + b
                for u in range(per):
                    e = (a * blocks + blk) * per + u
                    wu = writtens[blk][:, u * D : (u + 1) * D]
                    if b == 0:
                        now[hf, u] = jnp.concatenate([wu, th[e].astype(F32) + tl[e].astype(F32)], 1)
                    else:
                        now[hf, u] = dot_sf(th[e], tl[e], xs[hf, u]) + jnp.concatenate([wu, zero], 1)
                    if b < half - 1:
                        xsb[e] = jnp.concatenate(split(now[hf, u]), 0)
            xs = now
        for u in range(per):
            h = a * per + u
            for hf in range(2):
                xh[h * 2 + hf] = xs[hf, u]
            late = xs[1, u]
            xf[h] = dot_ff(late[:, D:], xs[0, u]) + jnp.concatenate([late[:, :D], zero], 1)

    def by_queries(a):
        hns, qns = [], []
        for blk in range(blocks):
            qq = qb[a, blk * B : (blk + 1) * B, :]
            qf = qq.astype(F32)
            qc = lax.rsqrt(jnp.sum(qf * qf, axis=1, keepdims=True) + 1e-6)
            hns.append(dot_t(qq, kb[a, blk * B : (blk + 1) * B, :]) * qc)
            qns.append(qf * qc)
        todo = []
        for blk in range(blocks):
            x = a * blocks + blk
            for u in range(per):
                e = x * per + u
                lr = dot_ef((wr[e] * hns[blk]).astype(BF), uw[e])
                far = (gates[x, :, 24 + u : 25 + u] * qns[blk] - lr[:, D:]).astype(BF)
                todo.append((blk, u, e, lr[:, :D], far))
        for blk, u, e, near, far in todo:
            if blk % half:
                o = dot(jnp.concatenate([far, far], 1), xsb[e - per])
                near = near + o[:, :D]
                far = o[:, D:].astype(BF)
            base[a * per + u, blk * B : (blk + 1) * B, :] = near
            r[a * per + u, blk * B : (blk + 1) * B, :] = far

    def chain(h):
        return pltpu.make_async_remote_copy(
            src_ref=sout.at[h],
            dst_ref=sin.at[h],
            send_sem=cs.at[h],
            recv_sem=cr.at[h],
            device_id={"ctx": lax.rem(c + pair, m)},
            device_id_type=MESH,
        )

    def send(h, s):
        device, dest = peer(s)
        return pltpu.make_async_remote_copy(
            src_ref=core.at[h, pl.ds(pl.multiple_of(dest * t, t), t), :],
            dst_ref=got.at[me * heads + h],
            send_sem=ss.at[h, s],
            recv_sem=rs.at[h, s],
            device_id=device,
            device_id_type=MESH,
        )

    def pass_on(h):
        @pl.when(z == 0)
        def _():
            sin[h] = jnp.zeros((D, D), F32)
            sout[h] = xf[h, :, :D]

        @pl.when(z > 0)
        def _():
            chain(h).wait_recv()

            @pl.when(z < zs - 1)
            def _():
                sout[h] = dot_ff(xf[h, :, D:], sin[h]) + xf[h, :, :D]

        @pl.when(z < zs - 1)
        def _():
            chain(h).start()

    def finish(h):
        mid = dot_ff(xh[h * 2, :, D:], sin[h]) + xh[h * 2, :, :D]
        for hf, s0 in enumerate((sin[h], mid)):
            rows = slice(hf * half * B, (hf + 1) * half * B)
            core[h, rows, :] = (base[h, rows, :] + dot_ef(r[h, rows, :], s0)).astype(BF)
        for s in range(1, group):
            send(h, s).start()

    scale = gain[...]
    gate_copy.wait()

    def gate_step(i, carry):
        cols = pl.ds(pl.multiple_of(i * D, D), D)
        g = gate[:, cols].astype(F32)
        gated[:, cols] = scale * (g / (1.0 + jnp.exp(-g)))
        return carry

    lax.fori_loop(0, heads * group, gate_step, 0)
    for i in range(2):
        small_local(i).wait()
        small_copy(i, n).wait_recv()
    for a in range(kheads):
        large_local(0, a).wait()
        large_copy(0, a, n).wait_recv()
    by_keys([(a, lax.rem(me + s, group)) for a in range(kheads) for s in (0, n)])
    for i in range(2):
        for s in others:
            small_copy(i, s).wait_recv()

    def keys_step(a, carry):
        for s in others:
            large_copy(0, a, s).wait_recv()
        by_keys([(a, lax.rem(me + s, group)) for s in others])
        return carry

    lax.fori_loop(0, kheads, keys_step, 0)

    def values_step(a, carry):
        arrive(1, a)
        by_values(a)

        @pl.when(jnp.where(a == 0, z <= 1, (z == 0) | (z == 2)))
        def _():
            for u in range(per):
                pass_on(jnp.where((a == 1) & (z == 0), per, 0) + u)

        return carry

    lax.fori_loop(0, kheads, values_step, 0)

    def queries_step(a, carry):
        arrive(2, a)
        by_queries(a)
        for u in range(per):
            h = a * per + u

            @pl.when(jnp.where(a == 0, z >= 3, z >= 2))
            def _():
                pass_on(h)

            finish(h)

        @pl.when((a == 0) & (z == 1))
        def _():
            for u in range(per):
                pass_on(per + u)

        return carry

    lax.fori_loop(0, kheads, queries_step, 0)

    def norm(i, x):
        x = x.astype(F32)
        cols = pl.ds(pl.multiple_of(i * D, D), D)
        y = x * lax.rsqrt(jnp.mean(x * x, axis=-1, keepdims=True) + 1e-6)
        out[:, cols] = (y * gated[:, cols]).astype(BF)

    def sent(a, carry):
        for i in range(3):
            for s in range(1, group):
                large_copy(i, a, s).wait_send()
        return carry

    lax.fori_loop(0, kheads, sent, 0)
    for i in range(2):
        for s in range(1, group):
            small_copy(i, s).wait_send()

    @pl.when(z < zs - 1)
    def _():
        for h in range(heads):
            chain(h).wait_send()

    def close(h, carry):
        norm(me * heads + h, core[h, mine, :])
        for s in range(1, group):
            send(h, s).wait_recv()
            i = lax.rem(me + group - s, group) * heads + h
            norm(i, got[i])
            send(h, s).wait_send()
        return carry

    lax.fori_loop(0, heads, close, 0)


def solution(mesh):
    n, m = mesh.shape["head"], mesh.shape["ctx"]
    pair = 2

    def local(q, k, v, gate, be, de, gain):
        t, width = v.shape
        group = n * pair
        heads = width // D // group
        kheads = k.shape[1] // D // group
        per = heads // kheads
        blocks = t * group // B
        wide = 16
        assert kheads == per == 2 and blocks == group and wide % heads == 0
        elems = heads * blocks
        vm = pl.BlockSpec(memory_space=pltpu.VMEM)
        hbm = pl.BlockSpec(memory_space=pl.ANY)
        dma = pltpu.SemaphoreType.DMA
        return pl.pallas_call(
            functools.partial(fused_kernel, n, m, pair, kheads, per),
            out_shape=pltpu.VMEM((t, width), BF),
            in_specs=[hbm] * 6 + [vm],
            out_specs=vm,
            scratch_shapes=[
                pltpu.VMEM((kheads, t * group, D), BF),
                pltpu.VMEM((kheads, t * group, D), BF),
                pltpu.VMEM((kheads, t * group, per * D), BF),
                pltpu.VMEM((group, wide, t), BF),
                pltpu.VMEM((group, wide, t), BF),
                pltpu.VMEM((t, width), BF),
                pltpu.VMEM((t, width), F32),
                pltpu.VMEM((elems, B, 2 * B), BF),
                pltpu.VMEM((elems, B, 2 * D), F32),
                pltpu.VMEM((elems, B, B), F32),
                pltpu.VMEM((elems, D, D), BF),
                pltpu.VMEM((elems, D, D), BF),
                pltpu.VMEM((kheads * blocks, D, B), BF),
                pltpu.VMEM((kheads * blocks, B, 32), F32),
                pltpu.VMEM((elems, 2 * D, 2 * D), BF),
                pltpu.VMEM((heads * 2, D, 2 * D), F32),
                pltpu.VMEM((heads, D, 2 * D), F32),
                pltpu.VMEM((heads, t * group, D), F32),
                pltpu.VMEM((heads, t * group, D), BF),
                pltpu.VMEM((heads, D, D), F32),
                pltpu.VMEM((heads, D, D), F32),
                pltpu.VMEM((heads, t * group, D), BF),
                pltpu.VMEM((heads * group, t, D), BF),
                dma((3, kheads, group)),
                dma((3, kheads, group)),
                dma((3, kheads)),
                dma((2, group)),
                dma((2, group)),
                dma((2,)),
                dma,
                dma((heads,)),
                dma((heads,)),
                dma((heads, group)),
                dma((heads, group)),
            ],
            compiler_params=pltpu.CompilerParams(
                collective_id=0, has_side_effects=True, vmem_limit_bytes=56 << 20
            ),
        )(q, k, v, be.T, de.T, gate, gain.reshape(1, D))

    rows = P(("ctx", "head"), None)
    return jax.shard_map(
        local, mesh=mesh, in_specs=(rows,) * 6 + (P(),), out_specs=rows, check_vma=False
    )
```

```python
import functools

import jax
import jax.numpy as jnp
from jax import lax
from jax.experimental import pallas as pl
from jax.experimental.pallas import tpu as pltpu
from jax.sharding import PartitionSpec as P

D = 128
B = 128
F32 = jnp.float32
BF = jnp.bfloat16
MESH = pl.DeviceIdType.MESH


def split(x):
    hi = x.astype(BF)
    return hi, (x - hi.astype(F32)).astype(BF)


def dot(a, b):
    return jnp.dot(a, b, preferred_element_type=F32)


def dot_t(a, b):
    return lax.dot_general(a, b, (((1,), (1,)), ((), ())), preferred_element_type=F32)


def dot_b(a, b):
    return dot(a.astype(BF), b.astype(BF))


def dot_fe(a, b):
    hi, lo = split(a)
    return dot(jnp.concatenate([hi, lo], 1), jnp.concatenate([b, b], 0))


def dot_ef(a, b):
    hi, lo = split(b)
    return dot(jnp.concatenate([a, a], 1), jnp.concatenate([hi, lo], 0))


def dot_sf(ah, al, b):
    bh, bl = split(b)
    return dot(jnp.concatenate([ah, ah], 1), jnp.concatenate([bh, bl], 0)) + dot(al, bh)


def dot_ff(a, b):
    return dot_sf(*split(a), b)


def odd_rows(x, w):
    return jnp.concatenate([x[i : i + w] for i in range(w, B, 2 * w)], 0)


def weave(even, odd, w):
    parts = []
    for i in range(0, B // 2, w):
        parts += [even[i : i + w], odd[i : i + w]]
    return jnp.concatenate(parts, 0)


def even_rows(x, w):
    return jnp.concatenate([x[i : i + w] for i in range(0, B, 2 * w)], 0)


def unit_lower_inverse(lows, ii, jj):
    eye = (ii == jj).astype(F32)
    base = (ii >> 4) == (jj >> 4)
    p = [jnp.where(base, -x, 0.0) for x in lows]
    pb = [x.astype(BF) for x in p]
    p2 = [dot(x, x) for x in pb]
    p2b = [x.astype(BF) for x in p2]
    z = [dot(x, jnp.concatenate([x, y], 1)) for x, y in zip(p2b, pb)]
    t = [eye + x + y + w[:, B:] for x, y, w in zip(p, p2, z)]
    p4b = [w[:, :B].astype(BF) for w in z]
    z = [dot(x, jnp.concatenate([x, y.astype(BF)], 1)) for x, y in zip(p4b, t)]
    t = [y + w[:, B:] for y, w in zip(t, z)]
    t = [y + dot(w[:, :B].astype(BF), y.astype(BF)) for y, w in zip(t, z)]
    w, bit = 16, 4
    zero = jnp.zeros((B // 2, B), BF)
    while w < B:
        below = odd_rows((ii >> bit) == (jj >> bit) + 1, w)
        tb = [y.astype(BF) for y in t]
        lo = [jnp.where(below, odd_rows(x, w), 0.0).astype(BF) for x in lows]
        z = [dot(x, y).astype(BF) for x, y in zip(lo, tb)]
        d = [dot(odd_rows(y, w), weave(zero, x, w)) for y, x in zip(tb, z)]
        t = [weave(even_rows(y, w), odd_rows(y, w) - x, w) for y, x in zip(t, d)]
        w, bit = 2 * w, bit + 1
    return t


def fused_kernel(
    n, m, pair, kheads, per,
    q, k, v, be, de, gate_hbm, gain,
    out,
    qb, kb, vb, own, packed, rows_in, gate, gated, ivs, uw, wr, th, tl, ktb, gates, xsb, xh, xf, base, r, sin, sout, core, got,
    es, er, el, fs, fr, fl, gs, cs, cr, ss, rs,
):
    hx = lax.axis_index("head")
    c = lax.axis_index("ctx")
    group = n * pair
    z = c // pair
    me = lax.rem(c, pair) * n + hx
    zs = m // pair
    heads = kheads * per
    t = q.shape[0]
    blocks = t * group // B
    half = blocks // 2

    def peer(s):
        rank = lax.rem(me + s, group)
        return {"ctx": z * pair + rank // n, "head": lax.rem(rank, n)}, rank

    barrier = pltpu.get_barrier_semaphore()
    for s in range(1, group):
        pl.semaphore_signal(barrier, inc=1, device_id=peer(s)[0], device_id_type=MESH)
    for s in (pair, m - pair):
        pl.semaphore_signal(barrier, inc=1, device_id={"ctx": lax.rem(c + s, m)}, device_id_type=MESH)
    mine = pl.ds(pl.multiple_of(me * t, t), t)
    large = ((k, kb, D), (v, vb, per * D), (q, qb, D))

    def small_copy(s):
        device, dest = peer(s)
        return pltpu.make_async_remote_copy(
            src_ref=packed.at[dest * heads // 8],
            dst_ref=rows_in.at[me],
            send_sem=fs.at[s],
            recv_sem=fr.at[s],
            device_id=device,
            device_id_type=MESH,
        )

    small_local = [pltpu.make_async_copy(x, own.at[i], fl.at[i]) for i, x in enumerate((de, be))]

    def piece(i, a, dest):
        w = large[i][2]
        return large[i][0].at[:, pl.ds(pl.multiple_of((dest * kheads + a) * w, w), w)]

    def large_copy(i, a, s):
        device, dest = peer(s)
        return pltpu.make_async_remote_copy(
            src_ref=piece(i, a, dest),
            dst_ref=large[i][1].at[a, mine, :],
            send_sem=es.at[i, a, s],
            recv_sem=er.at[i, a, s],
            device_id=device,
            device_id_type=MESH,
        )

    def large_local(i, a):
        return pltpu.make_async_copy(piece(i, a, me), large[i][1].at[a, mine, :], el.at[i, a])

    def arrive(i, a):
        for s in range(1, group):
            large_copy(i, a, s).wait_recv()
        large_local(i, a).wait()

    gate_copy = pltpu.make_async_copy(gate_hbm, gate, gs)
    gate_copy.start()
    for copy in small_local:
        copy.start()
    for a in range(kheads):
        large_local(0, a).start()
    pl.semaphore_wait(barrier, group + 1)
    others = [s for s in range(1, group) if s != n]
    for a in range(kheads):
        large_copy(0, a, n).start()
    for s in others:
        large_copy(0, 0, s).start()
    for copy in small_local:
        copy.wait()
    for j in range(packed.shape[0]):
        packed[j] = jnp.concatenate([own[0, j * 8 : j * 8 + 8, :], own[1, j * 8 : j * 8 + 8, :]], 0)
    for s in [n] + others:
        small_copy(s).start()
    rows_in[me] = packed[me * heads // 8]
    for s in others:
        large_copy(0, 1, s).start()
    for i in (1, 2):
        for a in range(kheads):
            for s in [n] + others:
                large_copy(i, a, s).start()
            large_local(i, a).start()

    ii = lax.broadcasted_iota(jnp.int32, (B, B), 0)
    jj = lax.broadcasted_iota(jnp.int32, (B, B), 1)
    eye = ii == jj
    causal = ii >= jj
    strict = ii > jj
    upp = (ii <= jj).astype(BF)

    def block_rows(blk):
        return pl.ds(pl.multiple_of(blk * B, B), B)

    def by_keys(items):
        first = lax.rem(me * heads, 8)
        idx = [a * blocks + blk for a, blk in items]
        drows, berows = [], []
        for a, blk in items:
            i8 = lax.broadcasted_iota(jnp.int32, (16, 16), 0)
            at = jnp.where((i8 & 7) < per, i8 + (first + a * per), -1)
            picked = dot((lax.broadcasted_iota(jnp.int32, (16, 16), 1) == at).astype(BF), rows_in[blk])
            drows.append(picked[:8].astype(BF))
            berows.append(picked[8:])
        kks = [kb[a, block_rows(blk), :] for a, blk in items]
        brows = [dot(x, upp) for x in drows]
        gs_ = [dot_t(x, x) for x in kks]
        kts = [jnp.transpose(x) for x in kks]
        rrs = [lax.rsqrt(jnp.sum(jnp.where(eye, x, 0.0), axis=0, keepdims=True) + 1e-6) for x in gs_]
        grs = [jnp.exp(x) for x in brows]
        turned = []
        for brow, grow, berow, rr in zip(brows, grs, berows, rrs):
            turned.append(jnp.concatenate([brow, jnp.exp(brow[:, B - 1 :] - brow) * rr, berow * rr, grow], 0))
        cols = []
        for i in range(0, len(items), 4):
            some = turned[i : i + 4]
            some += [some[-1]] * (4 - len(some))
            flat = jnp.transpose(jnp.concatenate(some, 0))
            cols += [flat[:, j * 32 : (j + 1) * 32] for j in range(4)]
        lows = []
        for x, col, kt, g, rr, brow in zip(idx, cols, kts, gs_, rrs, brows):
            ktb[x] = kt
            gates[x] = col
            gr = g * rr
            for u in range(per):
                gap = col[:, u : u + 1] - brow[u : u + 1, :]
                wts = jnp.where(causal, jnp.exp(jnp.minimum(gap, 0.0)), 0.0)
                lows.append(jnp.where(strict, col[:, 16 + u : 17 + u] * wts * gr, 0.0))
                wr[x * per + u] = wts * rr
        inv = unit_lower_inverse(lows, ii, jj)
        ws = []
        for i, (x, kk, berow, grow, rr) in enumerate(zip(idx, kks, berows, grs, rrs)):
            bgr = berow * grow * rr
            for u in range(per):
                y = inv[i * per + u]
                ivs[x * per + u] = jnp.concatenate(split(y * berow[u : u + 1, :]), 1)
                ws.append(dot_fe(y * bgr[u : u + 1, :], kk))
        downs = []
        for i, (x, kt, col) in enumerate(zip(idx, kts, cols)):
            ends = []
            for u in range(per):
                w = ws[i * per + u]
                uw[x * per + u, :, D:] = w
                ends.append(col[:, 8 + u : 9 + u] * w)
            downs.append(dot_ef(kt, jnp.concatenate(ends, 1)))
        for x, down, grow in zip(idx, downs, grs):
            for u in range(per):
                trans = jnp.where(eye, grow[u : u + 1, B - 1 :], 0.0) - down[:, u * D : (u + 1) * D]
                th[x * per + u], tl[x * per + u] = split(trans)

    zero = jnp.zeros((B, D), F32)

    def by_values(a):
        freshes = []
        for blk in range(blocks):
            for u in range(per):
                vv = vb[a, blk * B : (blk + 1) * B, u * D : (u + 1) * D]
                freshes.append(dot(ivs[(a * blocks + blk) * per + u], jnp.concatenate([vv, vv], 0)))
        writtens = []
        for blk in range(blocks):
            x = a * blocks + blk
            ends = []
            for u in range(per):
                fresh = freshes[blk * per + u]
                uw[x * per + u, :, :D] = fresh
                ends.append(gates[x, :, 8 + u : 9 + u] * fresh)
            writtens.append(dot_ef(ktb[x], jnp.concatenate(ends, 1)))
        xs = {}
        for b in range(half):
            now = {}
            for hf in range(2):
                blk = hf * half + b
                for u in range(per):
                    e = (a * blocks + blk) * per + u
                    wu = writtens[blk][:, u * D : (u + 1) * D]
                    if b == 0:
                        now[hf, u] = jnp.concatenate([wu, th[e].astype(F32) + tl[e].astype(F32)], 1)
                    else:
                        now[hf, u] = dot_sf(th[e], tl[e], xs[hf, u]) + jnp.concatenate([wu, zero], 1)
                    if b < half - 1:
                        xsb[e] = jnp.concatenate(split(now[hf, u]), 0)
            xs = now
        for u in range(per):
            h = a * per + u
            for hf in range(2):
                xh[h * 2 + hf] = xs[hf, u]
            late = xs[1, u]
            xf[h] = dot_ff(late[:, D:], xs[0, u]) + jnp.concatenate([late[:, :D], zero], 1)

    def by_queries(a):
        hns, qns = [], []
        for blk in range(blocks):
            qq = qb[a, blk * B : (blk + 1) * B, :]
            qf = qq.astype(F32)
            qc = lax.rsqrt(jnp.sum(qf * qf, axis=1, keepdims=True) + 1e-6)
            hns.append(dot_t(qq, kb[a, blk * B : (blk + 1) * B, :]) * qc)
            qns.append(qf * qc)
        todo = []
        for blk in range(blocks):
            x = a * blocks + blk
            for u in range(per):
                e = x * per + u
                lr = dot_ef((wr[e] * hns[blk]).astype(BF), uw[e])
                far = (gates[x, :, 24 + u : 25 + u] * qns[blk] - lr[:, D:]).astype(BF)
                todo.append((blk, u, e, lr[:, :D], far))
        for blk, u, e, near, far in todo:
            if blk % half:
                o = dot(jnp.concatenate([far, far], 1), xsb[e - per])
                near = near + o[:, :D]
                far = o[:, D:].astype(BF)
            base[a * per + u, blk * B : (blk + 1) * B, :] = near
            r[a * per + u, blk * B : (blk + 1) * B, :] = far

    def chain(h):
        return pltpu.make_async_remote_copy(
            src_ref=sout.at[h],
            dst_ref=sin.at[h],
            send_sem=cs.at[h],
            recv_sem=cr.at[h],
            device_id={"ctx": lax.rem(c + pair, m)},
            device_id_type=MESH,
        )

    def send(h, s):
        device, dest = peer(s)
        return pltpu.make_async_remote_copy(
            src_ref=core.at[h, pl.ds(pl.multiple_of(dest * t, t), t), :],
            dst_ref=got.at[me * heads + h],
            send_sem=ss.at[h, s],
            recv_sem=rs.at[h, s],
            device_id=device,
            device_id_type=MESH,
        )

    def pass_on(h):
        @pl.when(z == 0)
        def _():
            sin[h] = jnp.zeros((D, D), F32)
            sout[h] = xf[h, :, :D]

        @pl.when(z > 0)
        def _():
            chain(h).wait_recv()

            @pl.when(z < zs - 1)
            def _():
                sout[h] = dot_ff(xf[h, :, D:], sin[h]) + xf[h, :, :D]

        @pl.when(z < zs - 1)
        def _():
            chain(h).start()

    def finish(h):
        mid = dot_ff(xh[h * 2, :, D:], sin[h]) + xh[h * 2, :, :D]
        for hf, s0 in enumerate((sin[h], mid)):
            rows = slice(hf * half * B, (hf + 1) * half * B)
            core[h, rows, :] = (base[h, rows, :] + dot_ef(r[h, rows, :], s0)).astype(BF)
        for s in range(1, group):
            send(h, s).start()

    scale = gain[...]
    gate_copy.wait()

    def gate_step(i, carry):
        cols = pl.ds(pl.multiple_of(i * D, D), D)
        g = gate[:, cols].astype(F32)
        gated[:, cols] = scale * (g / (1.0 + jnp.exp(-g)))
        return carry

    lax.fori_loop(0, heads * group, gate_step, 0)
    small_copy(n).wait_recv()
    for a in range(kheads):
        large_local(0, a).wait()
        large_copy(0, a, n).wait_recv()
    by_keys([(a, lax.rem(me + s, group)) for a in range(kheads) for s in (0, n)])
    for s in others:
        small_copy(s).wait_recv()

    def keys_step(a, carry):
        for s in others:
            large_copy(0, a, s).wait_recv()
        by_keys([(a, lax.rem(me + s, group)) for s in others])
        return carry

    lax.fori_loop(0, kheads, keys_step, 0)

    def values_step(a, carry):
        arrive(1, a)
        by_values(a)

        @pl.when(jnp.where(a == 0, z <= 1, (z == 0) | (z == 2)))
        def _():
            for u in range(per):
                pass_on(jnp.where((a == 1) & (z == 0), per, 0) + u)

        return carry

    lax.fori_loop(0, kheads, values_step, 0)

    def queries_step(a, carry):
        arrive(2, a)
        by_queries(a)
        for u in range(per):
            h = a * per + u

            @pl.when(jnp.where(a == 0, z >= 3, z >= 2))
            def _():
                pass_on(h)

            finish(h)

        @pl.when((a == 0) & (z == 1))
        def _():
            for u in range(per):
                pass_on(per + u)

        return carry

    lax.fori_loop(0, kheads, queries_step, 0)

    def norm(i, x):
        x = x.astype(F32)
        cols = pl.ds(pl.multiple_of(i * D, D), D)
        y = x * lax.rsqrt(jnp.mean(x * x, axis=-1, keepdims=True) + 1e-6)
        out[:, cols] = (y * gated[:, cols]).astype(BF)

    def sent(a, carry):
        for i in range(3):
            for s in range(1, group):
                large_copy(i, a, s).wait_send()
        return carry

    lax.fori_loop(0, kheads, sent, 0)
    for s in range(1, group):
        small_copy(s).wait_send()

    @pl.when(z < zs - 1)
    def _():
        for h in range(heads):
            chain(h).wait_send()

    def close(h, carry):
        norm(me * heads + h, core[h, mine, :])
        for s in range(1, group):
            send(h, s).wait_recv()
            i = lax.rem(me + group - s, group) * heads + h
            norm(i, got[i])
            send(h, s).wait_send()
        return carry

    lax.fori_loop(0, heads, close, 0)


def solution(mesh):
    n, m = mesh.shape["head"], mesh.shape["ctx"]
    pair = 2

    def local(q, k, v, gate, be, de, gain):
        t, width = v.shape
        group = n * pair
        heads = width // D // group
        kheads = k.shape[1] // D // group
        per = heads // kheads
        blocks = t * group // B
        assert kheads == per == 2 and blocks == group and 8 % heads == 0
        elems = heads * blocks
        vm = pl.BlockSpec(memory_space=pltpu.VMEM)
        hbm = pl.BlockSpec(memory_space=pl.ANY)
        dma = pltpu.SemaphoreType.DMA
        return pl.pallas_call(
            functools.partial(fused_kernel, n, m, pair, kheads, per),
            out_shape=pltpu.VMEM((t, width), BF),
            in_specs=[hbm] * 6 + [vm],
            out_specs=vm,
            scratch_shapes=[
                pltpu.VMEM((kheads, t * group, D), BF),
                pltpu.VMEM((kheads, t * group, D), BF),
                pltpu.VMEM((kheads, t * group, per * D), BF),
                pltpu.VMEM((2, be.shape[1], t), BF),
                pltpu.VMEM((be.shape[1] // 8, 16, t), BF),
                pltpu.VMEM((group, 16, t), BF),
                pltpu.VMEM((t, width), BF),
                pltpu.VMEM((t, width), F32),
                pltpu.VMEM((elems, B, 2 * B), BF),
                pltpu.VMEM((elems, B, 2 * D), F32),
                pltpu.VMEM((elems, B, B), F32),
                pltpu.VMEM((elems, D, D), BF),
                pltpu.VMEM((elems, D, D), BF),
                pltpu.VMEM((kheads * blocks, D, B), BF),
                pltpu.VMEM((kheads * blocks, B, 32), F32),
                pltpu.VMEM((elems, 2 * D, 2 * D), BF),
                pltpu.VMEM((heads * 2, D, 2 * D), F32),
                pltpu.VMEM((heads, D, 2 * D), F32),
                pltpu.VMEM((heads, t * group, D), F32),
                pltpu.VMEM((heads, t * group, D), BF),
                pltpu.VMEM((heads, D, D), F32),
                pltpu.VMEM((heads, D, D), F32),
                pltpu.VMEM((heads, t * group, D), BF),
                pltpu.VMEM((heads * group, t, D), BF),
                dma((3, kheads, group)),
                dma((3, kheads, group)),
                dma((3, kheads)),
                dma((group,)),
                dma((group,)),
                dma((2,)),
                dma,
                dma((heads,)),
                dma((heads,)),
                dma((heads, group)),
                dma((heads, group)),
            ],
            compiler_params=pltpu.CompilerParams(
                collective_id=0, has_side_effects=True, vmem_limit_bytes=56 << 20
            ),
        )(q, k, v, be.T, de.T, gate, gain.reshape(1, D))

    rows = P(("ctx", "head"), None)
    return jax.shard_map(
        local, mesh=mesh, in_specs=(rows,) * 6 + (P(),), out_specs=rows, check_vma=False
    )
```

```python
import functools

import jax
import jax.numpy as jnp
from jax import lax
from jax.experimental import pallas as pl
from jax.experimental.pallas import tpu as pltpu
from jax.sharding import PartitionSpec as P

D = 128
B = 128
F32 = jnp.float32
BF = jnp.bfloat16
MESH = pl.DeviceIdType.MESH


def split(x):
    hi = x.astype(BF)
    return hi, (x - hi.astype(F32)).astype(BF)


def dot(a, b):
    return jnp.dot(a, b, preferred_element_type=F32)


def dot_t(a, b):
    return lax.dot_general(a, b, (((1,), (1,)), ((), ())), preferred_element_type=F32)


def dot_b(a, b):
    return dot(a.astype(BF), b.astype(BF))


def dot_fe(a, b):
    hi, lo = split(a)
    return dot(jnp.concatenate([hi, lo], 1), jnp.concatenate([b, b], 0))


def dot_ef(a, b):
    hi, lo = split(b)
    return dot(jnp.concatenate([a, a], 1), jnp.concatenate([hi, lo], 0))


def dot_sf(ah, al, b):
    bh, bl = split(b)
    return dot(jnp.concatenate([ah, ah], 1), jnp.concatenate([bh, bl], 0)) + dot(al, bh)


def dot_ff(a, b):
    return dot_sf(*split(a), b)


def odd_rows(x, w):
    return jnp.concatenate([x[i : i + w] for i in range(w, B, 2 * w)], 0)


def weave(even, odd, w):
    parts = []
    for i in range(0, B // 2, w):
        parts += [even[i : i + w], odd[i : i + w]]
    return jnp.concatenate(parts, 0)


def even_rows(x, w):
    return jnp.concatenate([x[i : i + w] for i in range(0, B, 2 * w)], 0)


def unit_lower_inverse(lows, ii, jj):
    eye = (ii == jj).astype(F32)
    base = (ii >> 4) == (jj >> 4)
    p = [jnp.where(base, -x, 0.0) for x in lows]
    pb = [x.astype(BF) for x in p]
    p2 = [dot(x, x) for x in pb]
    p2b = [x.astype(BF) for x in p2]
    z = [dot(x, jnp.concatenate([x, y], 1)) for x, y in zip(p2b, pb)]
    t = [eye + x + y + w[:, B:] for x, y, w in zip(p, p2, z)]
    p4b = [w[:, :B].astype(BF) for w in z]
    z = [dot(x, jnp.concatenate([x, y.astype(BF)], 1)) for x, y in zip(p4b, t)]
    t = [y + w[:, B:] for y, w in zip(t, z)]
    t = [y + dot(w[:, :B].astype(BF), y.astype(BF)) for y, w in zip(t, z)]
    w, bit = 16, 4
    zero = jnp.zeros((B // 2, B), BF)
    while w < B:
        below = odd_rows((ii >> bit) == (jj >> bit) + 1, w)
        tb = [y.astype(BF) for y in t]
        lo = [jnp.where(below, odd_rows(x, w), 0.0).astype(BF) for x in lows]
        z = [dot(x, y).astype(BF) for x, y in zip(lo, tb)]
        d = [dot(odd_rows(y, w), weave(zero, x, w)) for y, x in zip(tb, z)]
        t = [weave(even_rows(y, w), odd_rows(y, w) - x, w) for y, x in zip(t, d)]
        w, bit = 2 * w, bit + 1
    return t


def fused_kernel(
    n, m, pair, kheads, per,
    q, k, v, be, de, gate_hbm, gain,
    out,
    qb, kb, vb, own, packed, rows_in, gate, gated, ivs, uw, wr, th, tl, ktb, gates, xsb, xh, xf, base, r, sin, sout, core, got,
    es, er, el, fs, fr, fl, gs, cs, cr, ss, rs,
):
    hx = lax.axis_index("head")
    c = lax.axis_index("ctx")
    group = n * pair
    z = c // pair
    me = lax.rem(c, pair) * n + hx
    zs = m // pair
    heads = kheads * per
    t = q.shape[0]
    blocks = t * group // B
    half = blocks // 2

    def peer(s):
        rank = lax.rem(me + s, group)
        return {"ctx": z * pair + rank // n, "head": lax.rem(rank, n)}, rank

    barrier = pltpu.get_barrier_semaphore()
    for s in range(1, group):
        pl.semaphore_signal(barrier, inc=1, device_id=peer(s)[0], device_id_type=MESH)
    for s in (pair, m - pair):
        pl.semaphore_signal(barrier, inc=1, device_id={"ctx": lax.rem(c + s, m)}, device_id_type=MESH)
    mine = pl.ds(pl.multiple_of(me * t, t), t)
    large = ((k, kb, D), (v, vb, per * D), (q, qb, D))

    def small_copy(s):
        device, dest = peer(s)
        return pltpu.make_async_remote_copy(
            src_ref=packed.at[dest * heads // 8],
            dst_ref=rows_in.at[me],
            send_sem=fs.at[s],
            recv_sem=fr.at[s],
            device_id=device,
            device_id_type=MESH,
        )

    small_local = [pltpu.make_async_copy(x, own.at[i], fl.at[i]) for i, x in enumerate((de, be))]

    def piece(i, a, dest):
        w = large[i][2]
        return large[i][0].at[:, pl.ds(pl.multiple_of((dest * kheads + a) * w, w), w)]

    def large_copy(i, a, s):
        device, dest = peer(s)
        return pltpu.make_async_remote_copy(
            src_ref=piece(i, a, dest),
            dst_ref=large[i][1].at[a, mine, :],
            send_sem=es.at[i, a, s],
            recv_sem=er.at[i, a, s],
            device_id=device,
            device_id_type=MESH,
        )

    def large_local(i, a):
        return pltpu.make_async_copy(piece(i, a, me), large[i][1].at[a, mine, :], el.at[i, a])

    def arrive(i, a):
        for s in range(1, group):
            large_copy(i, a, s).wait_recv()
        large_local(i, a).wait()

    gate_copy = pltpu.make_async_copy(gate_hbm, gate, gs)
    gate_copy.start()
    for copy in small_local:
        copy.start()
    for a in range(kheads):
        large_local(0, a).start()
    pl.semaphore_wait(barrier, group + 1)
    others = [s for s in range(1, group) if s != n]
    for a in range(kheads):
        large_copy(0, a, n).start()
    for s in others:
        large_copy(0, 0, s).start()
    for copy in small_local:
        copy.wait()
    gate_rows = [own[i].astype(F32) for i in range(2)]
    for j in range(packed.shape[0]):
        packed[j] = jnp.concatenate([x[j * 8 : j * 8 + 8] for x in gate_rows], 0).astype(BF)
    for s in [n] + others:
        small_copy(s).start()
    rows_in[me] = packed[me * heads // 8]
    for s in others:
        large_copy(0, 1, s).start()
    for i in (1, 2):
        for a in range(kheads):
            for s in [n] + others:
                large_copy(i, a, s).start()
            large_local(i, a).start()

    ii = lax.broadcasted_iota(jnp.int32, (B, B), 0)
    jj = lax.broadcasted_iota(jnp.int32, (B, B), 1)
    eye = ii == jj
    causal = ii >= jj
    strict = ii > jj
    upp = (ii <= jj).astype(BF)

    def block_rows(blk):
        return pl.ds(pl.multiple_of(blk * B, B), B)

    def by_keys(items):
        first = lax.rem(me * heads, 8)
        idx = [a * blocks + blk for a, blk in items]
        drows, berows = [], []
        for a, blk in items:
            i8 = lax.broadcasted_iota(jnp.int32, (16, 16), 0)
            at = jnp.where((i8 & 7) < per, i8 + (first + a * per), -1)
            picked = dot((lax.broadcasted_iota(jnp.int32, (16, 16), 1) == at).astype(BF), rows_in[blk])
            drows.append(picked[:8].astype(BF))
            berows.append(picked[8:])
        kks = [kb[a, block_rows(blk), :] for a, blk in items]
        brows = [dot(x, upp) for x in drows]
        gs_ = [dot_t(x, x) for x in kks]
        kts = [jnp.transpose(x) for x in kks]
        rrs = [lax.rsqrt(jnp.sum(jnp.where(eye, x, 0.0), axis=0, keepdims=True) + 1e-6) for x in gs_]
        grs = [jnp.exp(x) for x in brows]
        turned = []
        for brow, grow, berow, rr in zip(brows, grs, berows, rrs):
            turned.append(jnp.concatenate([brow, jnp.exp(brow[:, B - 1 :] - brow) * rr, berow * rr, grow], 0))
        cols = []
        for i in range(0, len(items), 4):
            some = turned[i : i + 4]
            some += [some[-1]] * (4 - len(some))
            flat = jnp.transpose(jnp.concatenate(some, 0))
            cols += [flat[:, j * 32 : (j + 1) * 32] for j in range(4)]
        lows = []
        for x, col, kt, g, rr, brow in zip(idx, cols, kts, gs_, rrs, brows):
            ktb[x] = kt
            gates[x] = col
            gr = g * rr
            for u in range(per):
                gap = col[:, u : u + 1] - brow[u : u + 1, :]
                wts = jnp.where(causal, jnp.exp(jnp.minimum(gap, 0.0)), 0.0)
                lows.append(jnp.where(strict, col[:, 16 + u : 17 + u] * wts * gr, 0.0))
                wr[x * per + u] = wts * rr
        inv = unit_lower_inverse(lows, ii, jj)
        ws = []
        for i, (x, kk, berow, grow, rr) in enumerate(zip(idx, kks, berows, grs, rrs)):
            bgr = berow * grow * rr
            for u in range(per):
                y = inv[i * per + u]
                ivs[x * per + u] = jnp.concatenate(split(y * berow[u : u + 1, :]), 1)
                ws.append(dot_fe(y * bgr[u : u + 1, :], kk))
        downs = []
        for i, (x, kt, col) in enumerate(zip(idx, kts, cols)):
            ends = []
            for u in range(per):
                w = ws[i * per + u]
                uw[x * per + u, :, D:] = w
                ends.append(col[:, 8 + u : 9 + u] * w)
            downs.append(dot_ef(kt, jnp.concatenate(ends, 1)))
        for x, down, grow in zip(idx, downs, grs):
            for u in range(per):
                trans = jnp.where(eye, grow[u : u + 1, B - 1 :], 0.0) - down[:, u * D : (u + 1) * D]
                th[x * per + u], tl[x * per + u] = split(trans)

    zero = jnp.zeros((B, D), F32)

    def by_values(a):
        freshes = []
        for blk in range(blocks):
            for u in range(per):
                vv = vb[a, blk * B : (blk + 1) * B, u * D : (u + 1) * D]
                freshes.append(dot(ivs[(a * blocks + blk) * per + u], jnp.concatenate([vv, vv], 0)))
        writtens = []
        for blk in range(blocks):
            x = a * blocks + blk
            ends = []
            for u in range(per):
                fresh = freshes[blk * per + u]
                uw[x * per + u, :, :D] = fresh
                ends.append(gates[x, :, 8 + u : 9 + u] * fresh)
            writtens.append(dot_ef(ktb[x], jnp.concatenate(ends, 1)))
        xs = {}
        for b in range(half):
            now = {}
            for hf in range(2):
                blk = hf * half + b
                for u in range(per):
                    e = (a * blocks + blk) * per + u
                    wu = writtens[blk][:, u * D : (u + 1) * D]
                    if b == 0:
                        now[hf, u] = jnp.concatenate([wu, th[e].astype(F32) + tl[e].astype(F32)], 1)
                    else:
                        now[hf, u] = dot_sf(th[e], tl[e], xs[hf, u]) + jnp.concatenate([wu, zero], 1)
                    if b < half - 1:
                        xsb[e] = jnp.concatenate(split(now[hf, u]), 0)
            xs = now
        for u in range(per):
            h = a * per + u
            for hf in range(2):
                xh[h * 2 + hf] = xs[hf, u]
            late = xs[1, u]
            xf[h] = dot_ff(late[:, D:], xs[0, u]) + jnp.concatenate([late[:, :D], zero], 1)

    def by_queries(a):
        hns, qns = [], []
        for blk in range(blocks):
            qq = qb[a, blk * B : (blk + 1) * B, :]
            qf = qq.astype(F32)
            qc = lax.rsqrt(jnp.sum(qf * qf, axis=1, keepdims=True) + 1e-6)
            hns.append(dot_t(qq, kb[a, blk * B : (blk + 1) * B, :]) * qc)
            qns.append(qf * qc)
        todo = []
        for blk in range(blocks):
            x = a * blocks + blk
            for u in range(per):
                e = x * per + u
                lr = dot_ef((wr[e] * hns[blk]).astype(BF), uw[e])
                far = (gates[x, :, 24 + u : 25 + u] * qns[blk] - lr[:, D:]).astype(BF)
                todo.append((blk, u, e, lr[:, :D], far))
        for blk, u, e, near, far in todo:
            if blk % half:
                o = dot(jnp.concatenate([far, far], 1), xsb[e - per])
                near = near + o[:, :D]
                far = o[:, D:].astype(BF)
            base[a * per + u, blk * B : (blk + 1) * B, :] = near
            r[a * per + u, blk * B : (blk + 1) * B, :] = far

    def chain(h):
        return pltpu.make_async_remote_copy(
            src_ref=sout.at[h],
            dst_ref=sin.at[h],
            send_sem=cs.at[h],
            recv_sem=cr.at[h],
            device_id={"ctx": lax.rem(c + pair, m)},
            device_id_type=MESH,
        )

    def send(h, s):
        device, dest = peer(s)
        return pltpu.make_async_remote_copy(
            src_ref=core.at[h, pl.ds(pl.multiple_of(dest * t, t), t), :],
            dst_ref=got.at[me * heads + h],
            send_sem=ss.at[h, s],
            recv_sem=rs.at[h, s],
            device_id=device,
            device_id_type=MESH,
        )

    def pass_on(h):
        @pl.when(z == 0)
        def _():
            sin[h] = jnp.zeros((D, D), F32)
            sout[h] = xf[h, :, :D]

        @pl.when(z > 0)
        def _():
            chain(h).wait_recv()

            @pl.when(z < zs - 1)
            def _():
                sout[h] = dot_ff(xf[h, :, D:], sin[h]) + xf[h, :, :D]

        @pl.when(z < zs - 1)
        def _():
            chain(h).start()

    def finish(h):
        mid = dot_ff(xh[h * 2, :, D:], sin[h]) + xh[h * 2, :, :D]
        for hf, s0 in enumerate((sin[h], mid)):
            rows = slice(hf * half * B, (hf + 1) * half * B)
            core[h, rows, :] = (base[h, rows, :] + dot_ef(r[h, rows, :], s0)).astype(BF)
        for s in range(1, group):
            send(h, s).start()

    scale = gain[...]
    gate_copy.wait()

    def gate_step(i, carry):
        cols = pl.ds(pl.multiple_of(i * D, D), D)
        g = gate[:, cols].astype(F32)
        gated[:, cols] = scale * (g / (1.0 + jnp.exp(-g)))
        return carry

    lax.fori_loop(0, heads * group, gate_step, 0)
    small_copy(n).wait_recv()
    for a in range(kheads):
        large_local(0, a).wait()
        large_copy(0, a, n).wait_recv()
    by_keys([(a, lax.rem(me + s, group)) for a in range(kheads) for s in (0, n)])
    for s in others:
        small_copy(s).wait_recv()

    def keys_step(a, carry):
        for s in others:
            large_copy(0, a, s).wait_recv()
        by_keys([(a, lax.rem(me + s, group)) for s in others])
        return carry

    lax.fori_loop(0, kheads, keys_step, 0)

    def values_step(a, carry):
        arrive(1, a)
        by_values(a)

        @pl.when(jnp.where(a == 0, z <= 1, (z == 0) | (z == 2)))
        def _():
            for u in range(per):
                pass_on(jnp.where((a == 1) & (z == 0), per, 0) + u)

        return carry

    lax.fori_loop(0, kheads, values_step, 0)

    def queries_step(a, carry):
        arrive(2, a)
        by_queries(a)
        for u in range(per):
            h = a * per + u

            @pl.when(jnp.where(a == 0, z >= 3, z >= 2))
            def _():
                pass_on(h)

            finish(h)

        @pl.when((a == 0) & (z == 1))
        def _():
            for u in range(per):
                pass_on(per + u)

        return carry

    lax.fori_loop(0, kheads, queries_step, 0)

    def norm(i, x):
        x = x.astype(F32)
        cols = pl.ds(pl.multiple_of(i * D, D), D)
        y = x * lax.rsqrt(jnp.mean(x * x, axis=-1, keepdims=True) + 1e-6)
        out[:, cols] = (y * gated[:, cols]).astype(BF)

    def sent(a, carry):
        for i in range(3):
            for s in range(1, group):
                large_copy(i, a, s).wait_send()
        return carry

    lax.fori_loop(0, kheads, sent, 0)
    for s in range(1, group):
        small_copy(s).wait_send()

    @pl.when(z < zs - 1)
    def _():
        for h in range(heads):
            chain(h).wait_send()

    def close(h, carry):
        norm(me * heads + h, core[h, mine, :])
        for s in range(1, group):
            send(h, s).wait_recv()
            i = lax.rem(me + group - s, group) * heads + h
            norm(i, got[i])
            send(h, s).wait_send()
        return carry

    lax.fori_loop(0, heads, close, 0)


def solution(mesh):
    n, m = mesh.shape["head"], mesh.shape["ctx"]
    pair = 2

    def local(q, k, v, gate, be, de, gain):
        t, width = v.shape
        group = n * pair
        heads = width // D // group
        kheads = k.shape[1] // D // group
        per = heads // kheads
        blocks = t * group // B
        assert kheads == per == 2 and blocks == group and 8 % heads == 0
        elems = heads * blocks
        vm = pl.BlockSpec(memory_space=pltpu.VMEM)
        hbm = pl.BlockSpec(memory_space=pl.ANY)
        dma = pltpu.SemaphoreType.DMA
        return pl.pallas_call(
            functools.partial(fused_kernel, n, m, pair, kheads, per),
            out_shape=pltpu.VMEM((t, width), BF),
            in_specs=[hbm] * 6 + [vm],
            out_specs=vm,
            scratch_shapes=[
                pltpu.VMEM((kheads, t * group, D), BF),
                pltpu.VMEM((kheads, t * group, D), BF),
                pltpu.VMEM((kheads, t * group, per * D), BF),
                pltpu.VMEM((2, be.shape[1], t), BF),
                pltpu.VMEM((be.shape[1] // 8, 16, t), BF),
                pltpu.VMEM((group, 16, t), BF),
                pltpu.VMEM((t, width), BF),
                pltpu.VMEM((t, width), F32),
                pltpu.VMEM((elems, B, 2 * B), BF),
                pltpu.VMEM((elems, B, 2 * D), F32),
                pltpu.VMEM((elems, B, B), F32),
                pltpu.VMEM((elems, D, D), BF),
                pltpu.VMEM((elems, D, D), BF),
                pltpu.VMEM((kheads * blocks, D, B), BF),
                pltpu.VMEM((kheads * blocks, B, 32), F32),
                pltpu.VMEM((elems, 2 * D, 2 * D), BF),
                pltpu.VMEM((heads * 2, D, 2 * D), F32),
                pltpu.VMEM((heads, D, 2 * D), F32),
                pltpu.VMEM((heads, t * group, D), F32),
                pltpu.VMEM((heads, t * group, D), BF),
                pltpu.VMEM((heads, D, D), F32),
                pltpu.VMEM((heads, D, D), F32),
                pltpu.VMEM((heads, t * group, D), BF),
                pltpu.VMEM((heads * group, t, D), BF),
                dma((3, kheads, group)),
                dma((3, kheads, group)),
                dma((3, kheads)),
                dma((group,)),
                dma((group,)),
                dma((2,)),
                dma,
                dma((heads,)),
                dma((heads,)),
                dma((heads, group)),
                dma((heads, group)),
            ],
            compiler_params=pltpu.CompilerParams(
                collective_id=0, has_side_effects=True, vmem_limit_bytes=56 << 20
            ),
        )(q, k, v, be.T, de.T, gate, gain.reshape(1, D))

    rows = P(("ctx", "head"), None)
    return jax.shard_map(
        local, mesh=mesh, in_specs=(rows,) * 6 + (P(),), out_specs=rows, check_vma=False
    )
```

```python
import functools

import jax
import jax.numpy as jnp
from jax import lax
from jax.experimental import pallas as pl
from jax.experimental.pallas import tpu as pltpu
from jax.sharding import PartitionSpec as P

D = 128
B = 128
F32 = jnp.float32
BF = jnp.bfloat16
MESH = pl.DeviceIdType.MESH


def split(x):
    hi = x.astype(BF)
    return hi, (x - hi.astype(F32)).astype(BF)


def dot(a, b):
    return jnp.dot(a, b, preferred_element_type=F32)


def dot_t(a, b):
    return lax.dot_general(a, b, (((1,), (1,)), ((), ())), preferred_element_type=F32)


def dot_b(a, b):
    return dot(a.astype(BF), b.astype(BF))


def dot_fe(a, b):
    hi, lo = split(a)
    return dot(jnp.concatenate([hi, lo], 1), jnp.concatenate([b, b], 0))


def dot_ef(a, b):
    hi, lo = split(b)
    return dot(jnp.concatenate([a, a], 1), jnp.concatenate([hi, lo], 0))


def dot_sf(ah, al, b):
    bh, bl = split(b)
    return dot(jnp.concatenate([ah, ah], 1), jnp.concatenate([bh, bl], 0)) + dot(al, bh)


def dot_ff(a, b):
    return dot_sf(*split(a), b)


def odd_rows(x, w):
    return jnp.concatenate([x[i : i + w] for i in range(w, B, 2 * w)], 0)


def weave(even, odd, w):
    parts = []
    for i in range(0, B // 2, w):
        parts += [even[i : i + w], odd[i : i + w]]
    return jnp.concatenate(parts, 0)


def even_rows(x, w):
    return jnp.concatenate([x[i : i + w] for i in range(0, B, 2 * w)], 0)


def unit_lower_inverse(lows, ii, jj):
    eye = (ii == jj).astype(F32)
    base = (ii >> 4) == (jj >> 4)
    p = [jnp.where(base, -x, 0.0) for x in lows]
    pb = [x.astype(BF) for x in p]
    p2 = [dot(x, x) for x in pb]
    p2b = [x.astype(BF) for x in p2]
    z = [dot(x, jnp.concatenate([x, y], 1)) for x, y in zip(p2b, pb)]
    t = [eye + x + y + w[:, B:] for x, y, w in zip(p, p2, z)]
    p4b = [w[:, :B].astype(BF) for w in z]
    z = [dot(x, jnp.concatenate([x, y.astype(BF)], 1)) for x, y in zip(p4b, t)]
    t = [y + w[:, B:] for y, w in zip(t, z)]
    t = [y + dot(w[:, :B].astype(BF), y.astype(BF)) for y, w in zip(t, z)]
    w, bit = 16, 4
    zero = jnp.zeros((B // 2, B), BF)
    while w < B:
        below = odd_rows((ii >> bit) == (jj >> bit) + 1, w)
        tb = [y.astype(BF) for y in t]
        lo = [jnp.where(below, odd_rows(x, w), 0.0).astype(BF) for x in lows]
        z = [dot(x, y).astype(BF) for x, y in zip(lo, tb)]
        d = [dot(odd_rows(y, w), weave(zero, x, w)) for y, x in zip(tb, z)]
        t = [weave(even_rows(y, w), odd_rows(y, w) - x, w) for y, x in zip(t, d)]
        w, bit = 2 * w, bit + 1
    return t


def fused_kernel(
    n, m, pair, kheads, per,
    q, k, v, be, de, gate_hbm, gain,
    out,
    qb, kb, vb, own, packed, rows_in, gate, gated, ivs, uw, wr, th, tl, ktb, gates, xsb, xh, xf, base, r, sin, sout, core, got,
    es, er, el, fs, fr, fl, gs, cs, cr, ss, rs,
):
    hx = lax.axis_index("head")
    c = lax.axis_index("ctx")
    group = n * pair
    z = c // pair
    me = lax.rem(c, pair) * n + hx
    zs = m // pair
    heads = kheads * per
    t = q.shape[0]
    blocks = t * group // B
    half = blocks // 2

    def peer(s):
        rank = lax.rem(me + s, group)
        return {"ctx": z * pair + rank // n, "head": lax.rem(rank, n)}, rank

    barrier = pltpu.get_barrier_semaphore()
    for s in range(1, group):
        pl.semaphore_signal(barrier, inc=1, device_id=peer(s)[0], device_id_type=MESH)
    for s in (pair, m - pair):
        pl.semaphore_signal(barrier, inc=1, device_id={"ctx": lax.rem(c + s, m)}, device_id_type=MESH)
    mine = pl.ds(pl.multiple_of(me * t, t), t)
    large = ((k, kb, D), (v, vb, per * D), (q, qb, D))

    def small_copy(s):
        device, dest = peer(s)
        return pltpu.make_async_remote_copy(
            src_ref=packed.at[dest * heads // 8],
            dst_ref=rows_in.at[me],
            send_sem=fs.at[s],
            recv_sem=fr.at[s],
            device_id=device,
            device_id_type=MESH,
        )

    small_local = [pltpu.make_async_copy(x, own.at[i], fl.at[i]) for i, x in enumerate((de, be))]

    def piece(i, a, dest):
        w = large[i][2]
        return large[i][0].at[:, pl.ds(pl.multiple_of((dest * kheads + a) * w, w), w)]

    def large_copy(i, a, s):
        device, dest = peer(s)
        return pltpu.make_async_remote_copy(
            src_ref=piece(i, a, dest),
            dst_ref=large[i][1].at[a, mine, :],
            send_sem=es.at[i, a, s],
            recv_sem=er.at[i, a, s],
            device_id=device,
            device_id_type=MESH,
        )

    def large_local(i, a):
        return pltpu.make_async_copy(piece(i, a, me), large[i][1].at[a, mine, :], el.at[i, a])

    def arrive(i, a):
        for s in range(1, group):
            large_copy(i, a, s).wait_recv()
        large_local(i, a).wait()

    gate_copy = pltpu.make_async_copy(gate_hbm, gate, gs)
    gate_copy.start()
    for copy in small_local:
        copy.start()
    for a in range(kheads):
        large_local(0, a).start()
    pl.semaphore_wait(barrier, group + 1)
    others = [s for s in range(1, group) if s != n]
    for a in range(kheads):
        large_copy(0, a, n).start()
    for s in others:
        large_copy(0, 0, s).start()
    for copy in small_local:
        copy.wait()
    gate_rows = [own[i].astype(F32) for i in range(2)]
    for j in range(packed.shape[0]):
        packed[j] = jnp.concatenate([x[j * 8 : j * 8 + 8] for x in gate_rows], 0).astype(BF)
    for s in [n] + others:
        small_copy(s).start()
    rows_in[me] = packed[me * heads // 8]
    for s in others:
        large_copy(0, 1, s).start()
    for i in (1, 2):
        for a in range(kheads):
            for s in others + [n]:
                large_copy(i, a, s).start()
            large_local(i, a).start()

    ii = lax.broadcasted_iota(jnp.int32, (B, B), 0)
    jj = lax.broadcasted_iota(jnp.int32, (B, B), 1)
    eye = ii == jj
    causal = ii >= jj
    strict = ii > jj
    upp = (ii <= jj).astype(BF)

    def block_rows(blk):
        return pl.ds(pl.multiple_of(blk * B, B), B)

    def by_keys(items):
        first = lax.rem(me * heads, 8)
        idx = [a * blocks + blk for a, blk in items]
        drows, berows = [], []
        for a, blk in items:
            i8 = lax.broadcasted_iota(jnp.int32, (16, 16), 0)
            at = jnp.where((i8 & 7) < per, i8 + (first + a * per), -1)
            picked = dot((lax.broadcasted_iota(jnp.int32, (16, 16), 1) == at).astype(BF), rows_in[blk])
            drows.append(picked[:8].astype(BF))
            berows.append(picked[8:])
        kks = [kb[a, block_rows(blk), :] for a, blk in items]
        brows = [dot(x, upp) for x in drows]
        gs_ = [dot_t(x, x) for x in kks]
        kts = [jnp.transpose(x) for x in kks]
        rrs = [lax.rsqrt(jnp.sum(jnp.where(eye, x, 0.0), axis=0, keepdims=True) + 1e-6) for x in gs_]
        grs = [jnp.exp(x) for x in brows]
        turned = []
        for brow, grow, berow, rr in zip(brows, grs, berows, rrs):
            turned.append(jnp.concatenate([brow, jnp.exp(brow[:, B - 1 :] - brow) * rr, berow * rr, grow], 0))
        cols = []
        for i in range(0, len(items), 4):
            some = turned[i : i + 4]
            some += [some[-1]] * (4 - len(some))
            flat = jnp.transpose(jnp.concatenate(some, 0))
            cols += [flat[:, j * 32 : (j + 1) * 32] for j in range(4)]
        lows = []
        for x, col, kt, g, rr, brow in zip(idx, cols, kts, gs_, rrs, brows):
            ktb[x] = kt
            gates[x] = col
            gr = g * rr
            for u in range(per):
                gap = col[:, u : u + 1] - brow[u : u + 1, :]
                wts = jnp.where(causal, jnp.exp(jnp.minimum(gap, 0.0)), 0.0)
                lows.append(jnp.where(strict, col[:, 16 + u : 17 + u] * wts * gr, 0.0))
                wr[x * per + u] = wts * rr
        inv = unit_lower_inverse(lows, ii, jj)
        ws = []
        for i, (x, kk, berow, grow, rr) in enumerate(zip(idx, kks, berows, grs, rrs)):
            bgr = berow * grow * rr
            for u in range(per):
                y = inv[i * per + u]
                ivs[x * per + u] = jnp.concatenate(split(y * berow[u : u + 1, :]), 1)
                ws.append(dot_fe(y * bgr[u : u + 1, :], kk))
        downs = []
        for i, (x, kt, col) in enumerate(zip(idx, kts, cols)):
            ends = []
            for u in range(per):
                w = ws[i * per + u]
                uw[x * per + u, :, D:] = w
                ends.append(col[:, 8 + u : 9 + u] * w)
            downs.append(dot_ef(kt, jnp.concatenate(ends, 1)))
        for x, down, grow in zip(idx, downs, grs):
            for u in range(per):
                trans = jnp.where(eye, grow[u : u + 1, B - 1 :], 0.0) - down[:, u * D : (u + 1) * D]
                th[x * per + u], tl[x * per + u] = split(trans)

    zero = jnp.zeros((B, D), F32)

    def by_values(a):
        freshes = []
        for blk in range(blocks):
            for u in range(per):
                vv = vb[a, blk * B : (blk + 1) * B, u * D : (u + 1) * D]
                freshes.append(dot(ivs[(a * blocks + blk) * per + u], jnp.concatenate([vv, vv], 0)))
        writtens = []
        for blk in range(blocks):
            x = a * blocks + blk
            ends = []
            for u in range(per):
                fresh = freshes[blk * per + u]
                uw[x * per + u, :, :D] = fresh
                ends.append(gates[x, :, 8 + u : 9 + u] * fresh)
            writtens.append(dot_ef(ktb[x], jnp.concatenate(ends, 1)))
        xs = {}
        for b in range(half):
            now = {}
            for hf in range(2):
                blk = hf * half + b
                for u in range(per):
                    e = (a * blocks + blk) * per + u
                    wu = writtens[blk][:, u * D : (u + 1) * D]
                    if b == 0:
                        now[hf, u] = jnp.concatenate([wu, th[e].astype(F32) + tl[e].astype(F32)], 1)
                    else:
                        now[hf, u] = dot_sf(th[e], tl[e], xs[hf, u]) + jnp.concatenate([wu, zero], 1)
                    if b < half - 1:
                        xsb[e] = jnp.concatenate(split(now[hf, u]), 0)
            xs = now
        for u in range(per):
            h = a * per + u
            for hf in range(2):
                xh[h * 2 + hf] = xs[hf, u]
            late = xs[1, u]
            xf[h] = dot_ff(late[:, D:], xs[0, u]) + jnp.concatenate([late[:, :D], zero], 1)

    def by_queries(a):
        hns, qns = [], []
        for blk in range(blocks):
            qq = qb[a, blk * B : (blk + 1) * B, :]
            qf = qq.astype(F32)
            qc = lax.rsqrt(jnp.sum(qf * qf, axis=1, keepdims=True) + 1e-6)
            hns.append(dot_t(qq, kb[a, blk * B : (blk + 1) * B, :]) * qc)
            qns.append(qf * qc)
        todo = []
        for blk in range(blocks):
            x = a * blocks + blk
            for u in range(per):
                e = x * per + u
                lr = dot_ef((wr[e] * hns[blk]).astype(BF), uw[e])
                far = (gates[x, :, 24 + u : 25 + u] * qns[blk] - lr[:, D:]).astype(BF)
                todo.append((blk, u, e, lr[:, :D], far))
        for blk, u, e, near, far in todo:
            if blk % half:
                o = dot(jnp.concatenate([far, far], 1), xsb[e - per])
                near = near + o[:, :D]
                far = o[:, D:].astype(BF)
            base[a * per + u, blk * B : (blk + 1) * B, :] = near
            r[a * per + u, blk * B : (blk + 1) * B, :] = far

    def chain(h):
        return pltpu.make_async_remote_copy(
            src_ref=sout.at[h],
            dst_ref=sin.at[h],
            send_sem=cs.at[h],
            recv_sem=cr.at[h],
            device_id={"ctx": lax.rem(c + pair, m)},
            device_id_type=MESH,
        )

    def send(h, s):
        device, dest = peer(s)
        return pltpu.make_async_remote_copy(
            src_ref=core.at[h, pl.ds(pl.multiple_of(dest * t, t), t), :],
            dst_ref=got.at[me * heads + h],
            send_sem=ss.at[h, s],
            recv_sem=rs.at[h, s],
            device_id=device,
            device_id_type=MESH,
        )

    def pass_on(h):
        @pl.when(z == 0)
        def _():
            sin[h] = jnp.zeros((D, D), F32)
            sout[h] = xf[h, :, :D]

        @pl.when(z > 0)
        def _():
            chain(h).wait_recv()

            @pl.when(z < zs - 1)
            def _():
                sout[h] = dot_ff(xf[h, :, D:], sin[h]) + xf[h, :, :D]

        @pl.when(z < zs - 1)
        def _():
            chain(h).start()

    def finish(h):
        mid = dot_ff(xh[h * 2, :, D:], sin[h]) + xh[h * 2, :, :D]
        for hf, s0 in enumerate((sin[h], mid)):
            rows = slice(hf * half * B, (hf + 1) * half * B)
            core[h, rows, :] = (base[h, rows, :] + dot_ef(r[h, rows, :], s0)).astype(BF)
        for s in others + [n]:
            send(h, s).start()

    scale = gain[...]
    gate_copy.wait()

    def gate_step(i, carry):
        cols = pl.ds(pl.multiple_of(i * D, D), D)
        g = gate[:, cols].astype(F32)
        gated[:, cols] = scale * (g / (1.0 + jnp.exp(-g)))
        return carry

    lax.fori_loop(0, heads * group, gate_step, 0)
    small_copy(n).wait_recv()
    for a in range(kheads):
        large_local(0, a).wait()
        large_copy(0, a, n).wait_recv()
    by_keys([(a, lax.rem(me + s, group)) for a in range(kheads) for s in (0, n)])
    for s in others:
        small_copy(s).wait_recv()

    def keys_step(a, carry):
        for s in others:
            large_copy(0, a, s).wait_recv()
        by_keys([(a, lax.rem(me + s, group)) for s in others])
        return carry

    lax.fori_loop(0, kheads, keys_step, 0)

    def values_step(a, carry):
        arrive(1, a)
        by_values(a)

        @pl.when(jnp.where(a == 0, z <= 1, (z == 0) | (z == 2)))
        def _():
            for u in range(per):
                pass_on(jnp.where((a == 1) & (z == 0), per, 0) + u)

        return carry

    lax.fori_loop(0, kheads, values_step, 0)

    def queries_step(a, carry):
        arrive(2, a)
        by_queries(a)
        for u in range(per):
            h = a * per + u

            @pl.when(jnp.where(a == 0, z >= 3, z >= 2))
            def _():
                pass_on(h)

            finish(h)

        @pl.when((a == 0) & (z == 1))
        def _():
            for u in range(per):
                pass_on(per + u)

        return carry

    lax.fori_loop(0, kheads, queries_step, 0)

    def norm(i, x):
        x = x.astype(F32)
        cols = pl.ds(pl.multiple_of(i * D, D), D)
        y = x * lax.rsqrt(jnp.mean(x * x, axis=-1, keepdims=True) + 1e-6)
        out[:, cols] = (y * gated[:, cols]).astype(BF)

    def sent(a, carry):
        for i in range(3):
            for s in range(1, group):
                large_copy(i, a, s).wait_send()
        return carry

    lax.fori_loop(0, kheads, sent, 0)
    for s in range(1, group):
        small_copy(s).wait_send()

    @pl.when(z < zs - 1)
    def _():
        for h in range(heads):
            chain(h).wait_send()

    def close(h, carry):
        norm(me * heads + h, core[h, mine, :])
        for s in range(1, group):
            send(h, s).wait_recv()
            i = lax.rem(me + group - s, group) * heads + h
            norm(i, got[i])
            send(h, s).wait_send()
        return carry

    lax.fori_loop(0, heads, close, 0)


def solution(mesh):
    n, m = mesh.shape["head"], mesh.shape["ctx"]
    pair = 2

    def local(q, k, v, gate, be, de, gain):
        t, width = v.shape
        group = n * pair
        heads = width // D // group
        kheads = k.shape[1] // D // group
        per = heads // kheads
        blocks = t * group // B
        assert kheads == per == 2 and blocks == group and 8 % heads == 0
        elems = heads * blocks
        vm = pl.BlockSpec(memory_space=pltpu.VMEM)
        hbm = pl.BlockSpec(memory_space=pl.ANY)
        dma = pltpu.SemaphoreType.DMA
        return pl.pallas_call(
            functools.partial(fused_kernel, n, m, pair, kheads, per),
            out_shape=pltpu.VMEM((t, width), BF),
            in_specs=[hbm] * 6 + [vm],
            out_specs=vm,
            scratch_shapes=[
                pltpu.VMEM((kheads, t * group, D), BF),
                pltpu.VMEM((kheads, t * group, D), BF),
                pltpu.VMEM((kheads, t * group, per * D), BF),
                pltpu.VMEM((2, be.shape[1], t), BF),
                pltpu.VMEM((be.shape[1] // 8, 16, t), BF),
                pltpu.VMEM((group, 16, t), BF),
                pltpu.VMEM((t, width), BF),
                pltpu.VMEM((t, width), F32),
                pltpu.VMEM((elems, B, 2 * B), BF),
                pltpu.VMEM((elems, B, 2 * D), F32),
                pltpu.VMEM((elems, B, B), F32),
                pltpu.VMEM((elems, D, D), BF),
                pltpu.VMEM((elems, D, D), BF),
                pltpu.VMEM((kheads * blocks, D, B), BF),
                pltpu.VMEM((kheads * blocks, B, 32), F32),
                pltpu.VMEM((elems, 2 * D, 2 * D), BF),
                pltpu.VMEM((heads * 2, D, 2 * D), F32),
                pltpu.VMEM((heads, D, 2 * D), F32),
                pltpu.VMEM((heads, t * group, D), F32),
                pltpu.VMEM((heads, t * group, D), BF),
                pltpu.VMEM((heads, D, D), F32),
                pltpu.VMEM((heads, D, D), F32),
                pltpu.VMEM((heads, t * group, D), BF),
                pltpu.VMEM((heads * group, t, D), BF),
                dma((3, kheads, group)),
                dma((3, kheads, group)),
                dma((3, kheads)),
                dma((group,)),
                dma((group,)),
                dma((2,)),
                dma,
                dma((heads,)),
                dma((heads,)),
                dma((heads, group)),
                dma((heads, group)),
            ],
            compiler_params=pltpu.CompilerParams(
                collective_id=0, has_side_effects=True, vmem_limit_bytes=56 << 20
            ),
        )(q, k, v, be.T, de.T, gate, gain.reshape(1, D))

    rows = P(("ctx", "head"), None)
    return jax.shard_map(
        local, mesh=mesh, in_specs=(rows,) * 6 + (P(),), out_specs=rows, check_vma=False
    )
```
